128 devices in a mesh: genes: 64 (over x, z, y), batch: 2 (over core).
Axes of the slice: x: 4, y: 4, z: 4, core: 2. Of those that a mesh axis runs over, the one named last changes fastest.
Arguments:
- genotypes: bfloat16 [256, 3145728], P('batch', 'genes'), may hold values from 0 to 2, as said below
- gene_weight: bfloat16 [16, 3145728], P(None, 'genes'), may hold values from -0.375 to 0.375
- gene_lengths: int32 [12288], P('genes'), may hold values from 128 to 384, as said below
- membership: int32 [12288, 2], replicated, may hold values from 0 to 2047, as said below
- pathway_slot: int32 [2048], replicated, may hold values from 0 to 2047, as said below
- pathway_weight: bfloat16 [24576, 1024], P('genes'), may hold values from -0.4375 to 0.4375
- head_weight: bfloat16 [131072], P('genes'), may hold values from -0.75 to 0.75
- cotangent: float32 [256], P('batch'), may hold values from -3 to 3
Outputs:
- grad_gene: float32 [16, 3145728], P(None, 'genes')
- grad_pathway: float32 [24576, 1024], P('genes')
- grad_head: float32 [131072], P('genes')
The draws below stay inside these ranges and needn't reach their ends.
Inputs may be any that keep to these rules, and one draw needn't show every extreme that they name: `genotypes`: dosages 0, 1 or 2. `gene_lengths`: the 192 genes of each index of genes together hold exactly its 49152 variants. `membership`: the 2 pathways of a gene differ; of the links of one index's genes at most 12 go to pathways whose slots lie in one index's range of 32 slots, and some index receives exactly 12 from every index. `pathway_slot`: a permutation of the pathways; slot s is held by index s // 32 of genes.
All inputs are finite; a program needn't handle non-finite values.
Results may differ from the reference program's by a relative error of at most 0.0062.
Values may be sent and summed in bfloat16 or wider, within the bound.
A program may use at most 128 MiB of HBM per device.

```python
import math
import jax
import jax.numpy as jnp
from jax import lax

UNITS = 16
PUNITS = 64
MEMB = 2
GLEN = 256
GENE_DEV = 192
PATH_DEV = 32
SUBJECT_TOTAL = 256
GENES = 12288
VAR_DEV = 49152
VARIANTS = 3145728
EDGES_PER_SHARD = 384
EDGES = 24576
PATHWAYS = 2048
CAP = 12
N_GENES = 64


def draw_genotypes(key, part):
    freq_key = jax.random.fold_in(key, 1)
    pick_key = jax.random.fold_in(key, 2)
    minor_variant_share = jnp.exp(jax.random.uniform(freq_key, (1, VARIANTS), jnp.float32, math.log(0.03), math.log(0.5)))
    stochastic_uniform_values = jax.random.uniform(pick_key, (SUBJECT_TOTAL, VARIANTS), jnp.float32)
    holds_variant_flag = 1.0 - (1.0 - minor_variant_share) * (1.0 - minor_variant_share)
    variant_copies_matrix = (stochastic_uniform_values < holds_variant_flag).astype(jnp.float32) + (stochastic_uniform_values < minor_variant_share * minor_variant_share).astype(jnp.float32)
    return variant_copies_matrix.astype(jnp.bfloat16)


def draw_gene_lengths(key, part):
    device_count = GENES // GENE_DEV
    half_count = GENE_DEV // 2
    shift = jax.random.randint(jax.random.fold_in(key, 3), (device_count, half_count), -(GLEN // 2), GLEN // 2 + 1)
    shift = shift.at[:, 0].set(GLEN // 2)
    paired = jnp.concatenate([GLEN + shift, GLEN - shift], axis=1)
    scores = jax.random.randint(jax.random.fold_in(key, 4), (device_count, GENE_DEV), 0, 1 << 20) * GENE_DEV
    scores = scores + jnp.arange(GENE_DEV)[None, :]
    order = jnp.argsort(scores, axis=1)
    shuffled = jnp.take_along_axis(paired, order, axis=1)
    return shuffled.reshape(GENES).astype(jnp.int32)


def pathway_lookup(key):
    device_count = GENES // GENE_DEV
    slot_of = jax.random.permutation(jax.random.fold_in(key, 7), PATHWAYS).astype(jnp.int32)
    path_of = jnp.argsort(slot_of).astype(jnp.int32)
    hot_owner = jax.random.randint(jax.random.fold_in(key, 8), (), 0, device_count).astype(jnp.int32)

    def one_device(index):
        device_key = jax.random.fold_in(jax.random.fold_in(key, 9), index)
        cells = jnp.arange(device_count * CAP, dtype=jnp.int32)
        owners = cells // CAP
        scores = jax.random.permutation(jax.random.fold_in(device_key, 1), device_count * CAP).astype(jnp.int32)
        scores = scores + jnp.where(owners == hot_owner, device_count * CAP, 0).astype(jnp.int32)
        chosen = owners[jnp.argsort(scores)][:EDGES_PER_SHARD - CAP]
        targets = jnp.concatenate([jnp.full((CAP,), hot_owner, jnp.int32), chosen.astype(jnp.int32)])
        targets = targets[jax.random.permutation(jax.random.fold_in(device_key, 2), EDGES_PER_SHARD)]
        targets = targets.reshape(GENE_DEV, MEMB)
        first_local = jax.random.randint(jax.random.fold_in(device_key, 3), (GENE_DEV, 1), 0, PATH_DEV)
        step_local = jax.random.randint(jax.random.fold_in(device_key, 4), (GENE_DEV, 1), 1, PATH_DEV)
        local_index = jnp.concatenate([first_local, (first_local + step_local) % PATH_DEV], axis=1)
        return (targets * PATH_DEV + local_index).astype(jnp.int32)
    slots = jax.vmap(one_device)(jnp.arange(device_count, dtype=jnp.int32)).reshape(GENES, MEMB)
    return (slot_of, path_of[slots])


def draw_membership(key, part):
    return pathway_lookup(key)[1]


def draw_pathway_slot(key, part):
    return pathway_lookup(key)[0]


def steps_of(stream_key, shape, split, low, high):
    def one(dim, blocks):
        draws = jax.random.uniform(jax.random.fold_in(jax.random.fold_in(stream_key, 6), dim), (blocks,), jnp.float32, low / len(split), high / len(split))
        return jnp.repeat(jnp.exp(draws), shape[dim] // blocks).reshape((-1,) + (1,) * (len(shape) - dim - 1))

    loudness = one(*split[0])
    for cut in split[1:]:
        loudness = loudness * one(*cut)
    return loudness


def centred(rng, shape, width, bound, cuts=(), kind=jnp.bfloat16):
    drawn = width * jax.random.normal(rng, shape, jnp.float32)
    if cuts:
        drawn = drawn * steps_of(rng, shape, cuts, -0.22, 0.18)
    return jnp.clip(drawn, -bound, bound).astype(kind)


def setup_inputs(seed: int = 0) -> dict:
    key_of = jax.random.split(jax.random.key(seed), 9)
    return {
        "genotypes": draw_genotypes(jax.random.fold_in(key_of[8], 71), 0),
        "gene_weight": centred(key_of[1], (UNITS, VARIANTS), GLEN ** -0.5, 0.375, ((1, 64),)),
        "gene_lengths": draw_gene_lengths(jax.random.fold_in(key_of[8], 71), 0),
        "membership": draw_membership(jax.random.fold_in(key_of[8], 71), 0),
        "pathway_slot": draw_pathway_slot(jax.random.fold_in(key_of[8], 71), 0),
        "pathway_weight": centred(key_of[5], (EDGES, UNITS * PUNITS), 192 ** -0.5, 0.4375, ((0, 64),)),
        "head_weight": centred(key_of[6], (PATHWAYS * PUNITS,), PUNITS ** -0.5, 0.75, ((0, 64),)),
        "cotangent": centred(key_of[7], (SUBJECT_TOTAL,), 0.5, 3.0, ((0, 2),), jnp.float32),
    }


block_cols = 512


def gene_window_count():
    return block_cols // (GLEN // 2) + 2


def gene_windows(lengths, var_count, window):
    starts = (jnp.cumsum(lengths) - lengths).astype(jnp.int32)
    blocks = var_count // block_cols
    block_start = (jnp.arange(blocks) * block_cols).astype(jnp.int32)
    first_gene = (jnp.sum((starts[None, :] <= block_start[:, None]).astype(jnp.int32), axis=1) - 1).astype(jnp.int32)
    padded = jnp.concatenate([starts, jnp.full((window,), var_count, jnp.int32)])
    upcoming = padded[first_gene[:, None] + jnp.arange(1, window, dtype=jnp.int32)[None, :]]
    position = block_start[:, None] + jnp.arange(block_cols, dtype=jnp.int32)[None, :]
    which = jnp.sum((upcoming[:, None, :] <= position[:, :, None]).astype(jnp.int32), axis=2).astype(jnp.int32)
    select = which[:, None, :] == jnp.arange(window, dtype=jnp.int32)[None, :, None]
    gene_ids = first_gene[:, None] + jnp.arange(window, dtype=jnp.int32)[None, :]
    return gene_ids, select


def gene_forward(genotype_rows, weight_rows, lengths):
    samples, var_count = genotype_rows.shape
    unit_count = weight_rows.shape[0]
    window_genes = gene_window_count()
    gene_ids, select = gene_windows(lengths, var_count, window_genes)
    blocks = var_count // block_cols
    rows = genotype_rows.astype(jnp.float32).reshape(samples, blocks, block_cols)
    weight_blocks = weight_rows.astype(jnp.float32).reshape(unit_count, blocks, block_cols).transpose(1, 0, 2)
    basis = jnp.where(select[:, :, None, :], weight_blocks[:, None, :, :], jnp.zeros((), jnp.float32))
    basis = basis.reshape(blocks, window_genes * unit_count, block_cols)
    partial_sums = jnp.einsum("bkv,kcv->kcb", rows, basis)
    partial_sums = partial_sums.reshape(blocks * window_genes, unit_count, samples)
    preact = jax.ops.segment_sum(partial_sums, gene_ids.reshape(-1), num_segments=lengths.shape[0])
    return preact, gene_ids, select


def gene_backward(genotype_rows, preact_delta, gene_ids, select):
    samples, var_count = genotype_rows.shape
    gene_count, unit_count, _ = preact_delta.shape
    blocks = var_count // block_cols
    window = gene_ids.shape[1]
    rows = genotype_rows.astype(jnp.float32).reshape(samples, blocks, block_cols)
    windowed = preact_delta[jnp.minimum(gene_ids, gene_count - 1)].astype(jnp.float32)
    windowed = windowed.reshape(blocks, window * unit_count, samples)
    full_terms = jnp.einsum("bkv,kcb->kcv", rows, windowed).reshape(blocks, window, unit_count, block_cols)
    selected_entries = jnp.sum(jnp.where(select[:, :, None, :], full_terms, jnp.zeros((), jnp.float32)), axis=1)
    return selected_entries.transpose(1, 0, 2).reshape(unit_count, var_count)


def reference(genotypes, gene_weight, gene_lengths, membership, pathway_slot, pathway_weight, head_weight, cotangent):
    unit_count = gene_weight.shape[0]
    slots = pathway_slot[membership].astype(jnp.int32).reshape(-1)
    head_rows = head_weight.astype(jnp.float32).reshape(PATHWAYS, -1)
    path_units = head_rows.shape[1]
    link_weights = pathway_weight.reshape(EDGES, unit_count, path_units)
    shard_ids = jnp.arange(N_GENES, dtype=jnp.int32)

    def shard_inputs(index):
        rows = lax.dynamic_slice_in_dim(genotypes, index * VAR_DEV, VAR_DEV, 1)
        weight_rows = lax.dynamic_slice_in_dim(gene_weight, index * VAR_DEV, VAR_DEV, 1)
        lengths = lax.dynamic_slice_in_dim(gene_lengths, index * GENE_DEV, GENE_DEV, 0)
        link_rows = lax.dynamic_slice_in_dim(link_weights, index * EDGES_PER_SHARD, EDGES_PER_SHARD, 0)
        own_slots = lax.dynamic_slice_in_dim(slots, index * EDGES_PER_SHARD, EDGES_PER_SHARD, 0)
        return rows, weight_rows, lengths, link_rows, own_slots

    def forward_shard(totals, index):
        rows, weight_rows, lengths, link_rows, own_slots = shard_inputs(index)
        preact, gene_ids, select = gene_forward(rows, weight_rows, lengths)
        hidden = jnp.tanh(preact).astype(jnp.bfloat16)
        hidden_links = jnp.repeat(hidden, MEMB, axis=0).astype(jnp.float32)
        message = jnp.einsum("eub,euk->ekb", hidden_links, link_rows.astype(jnp.float32)).astype(jnp.bfloat16)
        message = lax.optimization_barrier(message).astype(jnp.float32)
        totals = totals + jax.ops.segment_sum(message, own_slots, num_segments=PATHWAYS)
        return totals, hidden

    start_sums = jnp.zeros((PATHWAYS, path_units, SUBJECT_TOTAL), jnp.float32)
    pathway_sum, hiddens = lax.scan(forward_shard, start_sums, shard_ids)
    active = jnp.tanh(pathway_sum)
    grad_head = jnp.sum(active * cotangent[None, None, :], axis=2).reshape(-1)
    pathway_delta = (cotangent[None, None, :] * head_rows[:, :, None] * (1.0 - active * active)).astype(jnp.bfloat16)

    def backward_shard(carry, inputs):
        index, hidden = inputs
        rows, weight_rows, lengths, link_rows, own_slots = shard_inputs(index)
        gene_ids, select = gene_windows(lengths, VAR_DEV, gene_window_count())
        link_delta_rows = pathway_delta[own_slots].astype(jnp.float32)
        hidden_links = jnp.repeat(hidden, MEMB, axis=0).astype(jnp.float32)
        grad_links = jnp.einsum("eub,ekb->euk", hidden_links, link_delta_rows).reshape(EDGES_PER_SHARD, -1)
        hidden_delta = jnp.einsum("euk,ekb->eub", link_rows.astype(jnp.float32), link_delta_rows)
        hidden_delta = jnp.sum(hidden_delta.reshape(GENE_DEV, MEMB, unit_count, SUBJECT_TOTAL), axis=1)
        latent_broad_matrix = hidden.astype(jnp.float32)
        preact_delta = (hidden_delta * (1.0 - latent_broad_matrix * latent_broad_matrix)).astype(jnp.bfloat16)
        grad_rows = gene_backward(rows, preact_delta, gene_ids, select)
        return carry, (grad_rows, grad_links)

    _, (gene_grads, link_grads) = lax.scan(backward_shard, jnp.zeros((), jnp.float32), (shard_ids, hiddens))
    grad_gene = gene_grads.transpose(1, 0, 2).reshape(unit_count, VARIANTS)
    grad_pathway = link_grads.reshape(EDGES, -1)
    return grad_gene, grad_pathway, grad_head
```

```python
import functools

import jax
import jax.numpy as jnp
from jax import lax
from jax.experimental import pallas as pl
from jax.experimental.pallas import tpu as pltpu
from jax.sharding import PartitionSpec as P

MESH = pl.DeviceIdType.MESH
F32 = jnp.float32
BF16 = jnp.bfloat16
I32 = jnp.int32

CAP = 12
HALF = CAP // 2
COLS = 256
STEP = 2048
GROUP = 32
MAX_GROUPS = 56
STRIDE = 27

ROW_SEND = 0
ROW_PERM = 12
ROW_SLOT = 26
ROW_RET = 28
ROW_START = 32
ROW_FIRST = 34
TAB_ROWS = 40


def iota(shape, dim):
    return lax.broadcasted_iota(I32, shape, dim)


def one(mask):
    return jnp.where(mask, 1.0, 0.0).astype(BF16)


def mm(left, right):
    return jnp.dot(left, right, preferred_element_type=F32)


def mm_tn(left, right):
    return lax.dot_general(left, right, (((0,), (0,)), ((), ())), preferred_element_type=F32)


def mm_nt(left, right):
    return lax.dot_general(left, right, (((1,), (1,)), ((), ())), preferred_element_type=F32)


def to_col(row, n):
    eye = iota((n, n), 0) == iota((n, n), 1)
    return jnp.sum(jnp.where(eye, jnp.broadcast_to(row, (n, n)), 0.0), axis=1, keepdims=True)


def to_row(col, n):
    eye = iota((n, n), 0) == iota((n, n), 1)
    return jnp.sum(jnp.where(eye, jnp.broadcast_to(col, (n, n)), 0.0), axis=0, keepdims=True)


def index_kernel(devs, genes, paths, mem_ref, slot_ref, len_ref, tab_ref, s_ref, own_ref):
    me = lax.axis_index("genes")
    per = genes
    table = slot_ref[...]
    halves = jnp.concatenate([table >> 5, table & 31], axis=0).astype(F32).astype(BF16)
    rows = table.shape[0]
    pair = 2 * per

    for m in range(2):
        def look(j, _, m=m):
            q = mem_ref[m : m + 1, pl.ds(pl.multiple_of(j * pair, 128), pair)]
            lane = q & 127
            which = q >> 7
            hot = one(jnp.broadcast_to(lane, (128, pair)) == iota((128, pair), 0))
            vals = mm(halves, hot)
            pick = jnp.broadcast_to(which, (rows, pair)) == iota((rows, pair), 0)
            owner = jnp.sum(jnp.where(pick, vals[:rows], 0.0), axis=0, keepdims=True)
            local = jnp.sum(jnp.where(pick, vals[rows:], 0.0), axis=0, keepdims=True)
            slot = owner * 32.0 + local
            s_ref[pl.ds(m * devs + 2 * j, 1), :] = slot[:, :per]
            s_ref[pl.ds(m * devs + 2 * j + 1, 1), :] = slot[:, per:]
            return 0

        lax.fori_loop(0, devs // 2, look, 0, unroll=4)

    tab_ref[...] = jnp.zeros((TAB_ROWS, 128), I32)
    slots = s_ref[...].astype(I32)
    mine = (slots >> 5) == me
    local = (slots & 31).astype(F32)
    upper = one(iota((per, per), 0) < iota((per, per), 1))
    before = mm(one(mine), upper)
    count = jnp.sum(jnp.where(mine, 1.0, 0.0), axis=1, keepdims=True)
    lead = jnp.concatenate([jnp.zeros((devs, 1), F32), count[:devs]], axis=0)
    rank = before + lead
    lower = one(iota((devs, devs), 1) < iota((devs, devs), 0))
    lane64 = iota((devs, 128), 1)
    carry = jnp.zeros((1, 128), F32)
    places, cells = [], []
    for r in range(CAP):
        hit = mine & (rank == float(r))
        got = jnp.sum(jnp.where(hit, local + 1.0, 0.0), axis=1, keepdims=True)
        got = got[:devs] + got[devs:]
        cell = jnp.where(got == 0.0, float(paths), got - 1.0).astype(I32)
        hot = jnp.broadcast_to(cell, (devs, 128)) == lane64
        within = mm(lower, one(hot)) + carry
        carry = carry + jnp.sum(jnp.where(hot, 1.0, 0.0), axis=0, keepdims=True)
        places.append(jnp.sum(jnp.where(hot, within, 0.0), axis=1, keepdims=True))
        cells.append(hot)
    lane1 = iota((1, 128), 1)
    groups = jnp.where(lane1 < paths, ((carry.astype(I32) + (GROUP - 1)) // GROUP).astype(F32), 0.0)
    strict = one(iota((128, 128), 0) < iota((128, 128), 1))
    start = mm(jnp.broadcast_to(groups.astype(BF16), (8, 128)), strict)[:1]
    end_col = to_col(start + groups, 128)
    ends = jnp.where(
        (jnp.broadcast_to(end_col, (128, 128)) <= iota((128, 128), 1).astype(F32))
        & (iota((128, 128), 0) < paths),
        1.0,
        0.0,
    )
    tab_ref[ROW_SLOT : ROW_SLOT + 1, :] = jnp.sum(ends, axis=0, keepdims=True).astype(I32)
    total = jnp.sum(groups, axis=1, keepdims=True)
    tab_ref[ROW_SLOT + 1 : ROW_SLOT + 2, :] = jnp.broadcast_to(total, (1, 128)).astype(I32)
    src_sum = jnp.zeros((16, 128), F32)
    rank_sum = jnp.zeros((16, 128), F32)
    seen = jnp.zeros((16, 128), F32)
    source = iota((devs, 128), 0).astype(F32).astype(BF16)
    for r in range(CAP):
        first = jnp.sum(
            jnp.where(cells[r], jnp.broadcast_to(start, (devs, 128)), 0.0), axis=1, keepdims=True
        )
        real = jnp.sum(jnp.where(cells[r] & (lane64 < paths), 1.0, 0.0), axis=1, keepdims=True)
        pos = (first * float(GROUP) + places[r]).astype(I32)
        pos = jnp.where(real > 0.0, pos, 1 << 20)
        high = one(jnp.broadcast_to(pos >> 7, (devs, 16)) == iota((devs, 16), 1))
        low = jnp.broadcast_to(pos & 127, (devs, 128)) == lane64
        src_sum = src_sum + mm_tn(high, jnp.where(low, source, jnp.zeros((), BF16)))
        found = mm_tn(high, one(low))
        rank_sum = rank_sum + found * float(r)
        seen = seen + found
    perm = jnp.where(seen > 0.0, src_sum * float(CAP) + rank_sum, float(devs * CAP))
    tab_ref[ROW_PERM : ROW_PERM + 14, :] = perm.astype(I32)[:14]

    own_ref[0:1, :] = s_ref[pl.ds(me, 1), :]
    own_ref[1:2, :] = s_ref[pl.ds(devs + me, 1), :]
    lower_g = one(iota((per, per), 1) < iota((per, per), 0))
    lane_g = iota((per, 128), 1)
    gene_col = iota((per, 128), 0).astype(F32).astype(BF16)
    carry = jnp.zeros((1, 128), F32)
    send = jnp.zeros((16, 128), F32)
    for m in range(2):
        owner = (to_col(own_ref[m : m + 1, :], per).astype(I32)) >> 5
        hot = jnp.broadcast_to(owner, (per, 128)) == lane_g
        within = mm(lower_g, one(hot)) + carry
        carry = carry + jnp.sum(jnp.where(hot, 1.0, 0.0), axis=0, keepdims=True)
        order = jnp.sum(jnp.where(hot, within, 0.0), axis=1, keepdims=True)
        cell = one(jnp.broadcast_to(order, (per, 16)) == iota((per, 16), 1).astype(F32))
        send = send + 2.0 * mm_tn(cell, jnp.where(hot, gene_col, jnp.zeros((), BF16)))
        if m:
            send = send + mm_tn(cell, one(hot))
        back = to_row(owner.astype(F32) * float(CAP) + order, per).astype(I32)
        tab_ref[ROW_RET + 2 * m : ROW_RET + 2 * m + 1, :] = back[:, :128]
        tab_ref[ROW_RET + 2 * m + 1 : ROW_RET + 2 * m + 2, : per - 128] = back[:, 128:]
    tab_ref[ROW_SEND : ROW_SEND + CAP, :] = send.astype(I32)[:CAP]

    lens = len_ref[...].astype(F32) - 128.0
    starts = mm(jnp.broadcast_to(lens.astype(BF16), (8, per)), upper)[:1]
    starts = starts + 128.0 * iota((1, per), 1).astype(F32)
    tab_ref[ROW_START : ROW_START + 1, :] = starts[:, :128].astype(I32)
    var_count = per * COLS
    tab_ref[ROW_START + 1 : ROW_START + 2, :] = jnp.full((1, 128), var_count, I32)
    tab_ref[ROW_START + 1 : ROW_START + 2, : per - 128] = starts[:, 128:].astype(I32)
    start_col = to_col(starts, per)
    begin = (iota((per, 256), 1) * COLS).astype(F32)
    inside = jnp.where(jnp.broadcast_to(start_col, (per, 256)) <= begin, 1.0, 0.0)
    first = (jnp.sum(inside, axis=0, keepdims=True) - 1.0).astype(I32)
    tab_ref[ROW_FIRST : ROW_FIRST + 1, :] = first[:, :128]
    tab_ref[ROW_FIRST + 1 : ROW_FIRST + 2, :] = first[:, 128:]


def look_up(tab_ref, row, index):
    return tab_ref[row + (index >> 7), index & 127]


def window_of(tab_ref, block):
    first = look_up(tab_ref, ROW_FIRST, block)
    one_end = look_up(tab_ref, ROW_START, first + 1) - block * COLS
    two_end = look_up(tab_ref, ROW_START, first + 2) - block * COLS
    return first, one_end, two_end


def forward_kernel(genes, units, tab_ref, geno_ref, weight_ref, hid_ref, acc_ref):
    step = pl.program_id(0)

    @pl.when(step == 0)
    def _():
        acc_ref[...] = jnp.zeros_like(acc_ref)

    pos = iota((units, COLS), 1)
    for k in range(STEP // COLS):
        first, one_end, two_end = window_of(tab_ref, step * (STEP // COLS) + k)
        weight = weight_ref[:, k * COLS : (k + 1) * COLS].astype(F32)
        not_one = pos >= one_end
        not_two = pos >= two_end
        zero = jnp.zeros_like(weight)
        basis = jnp.concatenate(
            [
                jnp.where(not_one, zero, weight),
                jnp.where(not_one & jnp.logical_not(not_two), weight, zero),
                jnp.where(not_two, weight, zero),
            ],
            axis=0,
        ).astype(BF16)
        part = mm_nt(basis, geno_ref[:, k * COLS : (k + 1) * COLS])
        rows = pl.ds(pl.multiple_of(first * units, units), 3 * units)
        acc_ref[rows, :] = acc_ref[rows, :] + part

    @pl.when(step == pl.num_programs(0) - 1)
    def _():
        def finish(g, _):
            base = g * units
            even = acc_ref[pl.ds(base, units // 2, stride=2), :]
            odd = acc_ref[pl.ds(base + 1, units // 2, stride=2), :]
            hid_ref[g] = jnp.tanh(jnp.concatenate([even, odd], axis=1)).astype(BF16)
            return 0

        lax.fori_loop(0, genes, finish, 0, unroll=8)


def partner(me, k):
    off = lax.rem(k * STRIDE, 64)
    x = lax.rem(me // 16 + off // 16, 4)
    z = lax.rem((me // 4) % 4 + (off // 4) % 4, 4)
    y = lax.rem(me % 4 + off % 4, 4)
    return x * 16 + z * 4 + y


def greet(devs, me, core):
    barrier = pltpu.get_barrier_semaphore()

    def hello(k, _):
        pl.semaphore_signal(
            barrier, inc=1, device_id=(partner(me, k), core), device_id_type=MESH
        )
        return 0

    lax.fori_loop(1, devs, hello, 0)
    pl.semaphore_signal(barrier, inc=1, device_id=(me, 1 - core), device_id_type=MESH)
    pl.semaphore_wait(barrier, devs)


def send_kernel(
    devs, tab_ref, hid_ref, link_ref, geno_ref, h_ref, w_ref, sib_ref,
    hs_ref, ws_ref, hsend, hrecv, wsend, wrecv, pair_sem, geno_sem,
):
    me = lax.axis_index("genes")
    core = lax.axis_index("batch")
    low = core * HALF
    greet(devs, me, core)
    geno = pltpu.make_async_remote_copy(
        src_ref=geno_ref, dst_ref=sib_ref, send_sem=geno_sem.at[0], recv_sem=geno_sem.at[1],
        device_id=(me, 1 - core), device_id_type=MESH,
    )
    geno.start()

    def w_copy(k):
        to = partner(me, k)
        return pltpu.make_async_remote_copy(
            src_ref=ws_ref.at[to], dst_ref=w_ref.at[me, pl.ds(low, HALF)],
            send_sem=wsend.at[k], recv_sem=wrecv.at[k],
            device_id=(to, core), device_id_type=MESH,
        )

    def h_copy(k):
        to = partner(me, k)
        return pltpu.make_async_remote_copy(
            src_ref=hs_ref.at[to], dst_ref=h_ref.at[me],
            send_sem=hsend.at[k], recv_sem=hrecv.at[k],
            device_id=(to, core), device_id_type=MESH,
        )

    def w_step(k, _):
        to = partner(me, k)
        for r in range(HALF):
            ws_ref[to, r] = link_ref[tab_ref[low + r, to]]
        w_copy(k).start()
        return 0

    lax.fori_loop(1, devs, w_step, 0)

    def h_step(k, _):
        to = partner(me, k)
        for r in range(CAP):
            hs_ref[to, r] = hid_ref[tab_ref[r, to] >> 1]
        h_copy(k).start()
        return 0

    lax.fori_loop(1, devs, h_step, 0)
    for r in range(CAP):
        h_ref[me, r] = hid_ref[tab_ref[r, me] >> 1]
    for r in range(HALF):
        w_ref[me, low + r] = link_ref[tab_ref[low + r, me]]
    h_ref[devs] = jnp.zeros(h_ref.shape[1:], BF16)
    w_ref[devs] = jnp.zeros(w_ref.shape[1:], BF16)

    def w_wait(k, _):
        w_copy(k).wait()
        return 0

    lax.fori_loop(1, devs, w_wait, 0)
    part = w_ref.at[pl.ds(0, devs), pl.ds(low, HALF)]
    share = pltpu.make_async_remote_copy(
        src_ref=part, dst_ref=part, send_sem=pair_sem.at[0], recv_sem=pair_sem.at[1],
        device_id=(me, 1 - core), device_id_type=MESH,
    )
    share.start()

    def h_wait(k, _):
        h_copy(k).wait()
        return 0

    lax.fori_loop(1, devs, h_wait, 0)
    share.wait()
    geno.wait()


def path_kernel(
    paths, punits, tab_ref, h_ref, w_ref, head_ref, cot_ref, hd_ref, gp_ref, gh_ref,
    hs_ref, ws_ref, sum_ref, delta_ref,
):
    total = tab_ref[ROW_SLOT + 1, 0]
    pairs = (total + 1) // 2
    sum_ref[...] = jnp.zeros_like(sum_ref)
    wide = 8 * GROUP

    def up(i, _):
        for half in range(2):
            c = 2 * i + half
            for j in range(GROUP):
                p = look_up(tab_ref, ROW_PERM, c * GROUP + j)
                hs_ref[c, pl.ds(8 * j, 8), :] = h_ref[p]
                ws_ref[c, pl.ds(8 * j, 8), :] = w_ref[p]
        for half in range(2):
            c = 2 * i + half
            slot = tab_ref[ROW_SLOT, c]
            out = mm_tn(ws_ref[c], hs_ref[c])
            sum_ref[slot] = sum_ref[slot] + out[:punits, :128] + out[punits:, 128:]
        return 0

    lax.fori_loop(0, pairs, up, 0)

    cot = cot_ref[...]
    lane = iota((punits, 128), 1)
    sub = iota((punits, 128), 0)

    def middle(i, _):
        row = jnp.zeros((1, 128), F32)
        head_row = head_ref[pl.ds(i, 1), :]
        for half in range(2):
            s = 2 * i + half
            active = jnp.tanh(sum_ref[s])
            diag = lane == sub + punits * half
            head = jnp.sum(
                jnp.where(diag, jnp.broadcast_to(head_row, (punits, 128)), 0.0),
                axis=1, keepdims=True,
            )
            grad = jnp.sum(active * cot, axis=1, keepdims=True)
            row = row + jnp.sum(
                jnp.where(diag, jnp.broadcast_to(grad, (punits, 128)), 0.0), axis=0, keepdims=True
            )
            delta = (cot * head * (1.0 - active * active)).astype(BF16)
            none = jnp.zeros_like(delta)
            delta_ref[s] = jnp.concatenate(
                [
                    jnp.concatenate([delta, none], axis=1),
                    jnp.concatenate([none, delta], axis=1),
                ],
                axis=0,
            )
        gh_ref[pl.ds(i, 1), :] = row
        return 0

    lax.fori_loop(0, paths // 2, middle, 0)
    delta_ref[paths] = jnp.zeros(delta_ref.shape[1:], BF16)

    def down(i, _):
        for half in range(2):
            c = 2 * i + half
            block = delta_ref[tab_ref[ROW_SLOT, c]]
            hd = mm(ws_ref[c], block).astype(BF16)
            gp = mm_nt(hs_ref[c], block)
            for j in range(GROUP):
                p = look_up(tab_ref, ROW_PERM, c * GROUP + j)
                hd_ref[p] = hd[8 * j : 8 * j + 8]
                gp_ref[p] = gp[8 * j : 8 * j + 8]
        return 0

    lax.fori_loop(0, pairs, down, 0)


def return_kernel(
    devs, genes, units, tab_ref, hd_ref, gp_ref, gh_ref, hid_ref,
    own_ref, sib_ref, link_ref, head_ref,
    back_ref, part_ref, gs_ref, ghs_ref, pd_ref,
    hsend, hrecv, gsend, grecv, pair_sem,
):
    me = lax.axis_index("genes")
    core = lax.axis_index("batch")
    low = core * HALF
    other = (1 - core) * HALF
    greet(devs, me, core)

    def pair(src, dst, n):
        return pltpu.make_async_remote_copy(
            src_ref=src, dst_ref=dst, send_sem=pair_sem.at[2 * n], recv_sem=pair_sem.at[2 * n + 1],
            device_id=(me, 1 - core), device_id_type=MESH,
        )

    def h_copy(k):
        to = partner(me, k)
        return pltpu.make_async_remote_copy(
            src_ref=hd_ref.at[to], dst_ref=back_ref.at[me],
            send_sem=hsend.at[k], recv_sem=hrecv.at[k],
            device_id=(to, core), device_id_type=MESH,
        )

    def g_copy(k):
        to = partner(me, k)
        return pltpu.make_async_remote_copy(
            src_ref=gs_ref.at[to], dst_ref=link_ref.at[me, pl.ds(low, HALF)],
            send_sem=gsend.at[k], recv_sem=grecv.at[k],
            device_id=(to, core), device_id_type=MESH,
        )

    def h_step(k, _):
        h_copy(k).start()
        return 0

    lax.fori_loop(1, devs, h_step, 0)
    parts = pair(gp_ref.at[pl.ds(0, devs), pl.ds(other, HALF)], part_ref, 0)
    parts.start()
    heads = pair(gh_ref, ghs_ref, 1)
    heads.start()
    back_ref[me] = hd_ref[me]
    parts.wait()

    def g_step(k, _):
        to = partner(me, k)
        gs_ref[to] = (gp_ref[to, pl.ds(low, HALF)] + part_ref[to]).astype(BF16)
        g_copy(k).start()
        return 0

    lax.fori_loop(1, devs, g_step, 0)
    link_ref[me, pl.ds(low, HALF)] = (gp_ref[me, pl.ds(low, HALF)] + part_ref[me]).astype(BF16)
    heads.wait()
    head_ref[...] = gh_ref[...] + ghs_ref[...]

    def h_wait(k, _):
        h_copy(k).wait()
        return 0

    lax.fori_loop(1, devs, h_wait, 0)

    def gene(g, _):
        a = look_up(tab_ref, ROW_RET, g)
        b = look_up(tab_ref, ROW_RET + 2, g)
        both = (
            back_ref[a // CAP, a % CAP].astype(F32) + back_ref[b // CAP, b % CAP].astype(F32)
        )
        hid = hid_ref[g].astype(F32)
        value = both * (1.0 - hid * hid)
        base = g * units
        pd_ref[pl.ds(base, units // 2, stride=2), :] = value[:, :128]
        pd_ref[pl.ds(base + 1, units // 2, stride=2), :] = value[:, 128:]
        return 0

    lax.fori_loop(0, genes, gene, 0, unroll=4)
    pad = own_ref.shape[0] - genes * units
    own_ref[pl.ds(0, genes * units), :] = pd_ref[...].astype(BF16)
    own_ref[pl.ds(genes * units, pad), :] = jnp.zeros((pad, 128), BF16)
    deltas = pair(own_ref, sib_ref, 2)
    deltas.start()

    def g_wait(k, _):
        g_copy(k).wait()
        return 0

    lax.fori_loop(1, devs, g_wait, 0)
    mine = link_ref.at[pl.ds(0, devs), pl.ds(low, HALF)]
    share = pair(mine, mine, 3)
    share.start()
    deltas.wait()
    share.wait()


def backward_kernel(
    units, tab_ref, own_ref, sib_ref, pd_own, pd_sib, link_ref, out_ref, gp_ref, gp_scr
):
    step = pl.program_id(0)
    links = gp_ref.shape[0]
    for j in range(links):
        g = step * (links // 2) + j // 2
        p = look_up(tab_ref, ROW_RET + 2 * (j % 2), g)
        gp_scr[pl.ds(8 * j, 8), :] = link_ref[p].astype(F32)
    for e in range(links // 8):
        for t in range(8):
            gp_ref[8 * e : 8 * e + 8, 128 * t : 128 * t + 128] = gp_scr[
                pl.ds(64 * e + t, 8, stride=8), :
            ]
    pos = iota((units, COLS), 1)
    for k in range(STEP // COLS):
        first, one_end, two_end = window_of(tab_ref, step * (STEP // COLS) + k)
        rows = pl.ds(pl.multiple_of(first * units, units), 3 * units)
        left = jnp.concatenate([pd_own[rows, :], pd_sib[rows, :]], axis=1)
        cols = slice(k * COLS, (k + 1) * COLS)
        right = jnp.concatenate([own_ref[:, cols], sib_ref[:, cols]], axis=0)
        full = mm(left, right)
        out_ref[:, cols] = jnp.where(
            pos >= two_end,
            full[2 * units :],
            jnp.where(pos >= one_end, full[units : 2 * units], full[:units]),
        )


def vmem():
    return pl.BlockSpec(memory_space=pltpu.VMEM)


def smem():
    return pl.BlockSpec(memory_space=pltpu.SMEM)


def hbm():
    return pl.BlockSpec(memory_space=pl.ANY)


LIMIT = 60 * 1024 * 1024


def on_device(
    genotypes, gene_weight, gene_lengths, membership, pathway_slot, pathway_weight,
    head_weight, cotangent,
):
    devs = lax.axis_size("genes")
    genes = gene_lengths.shape[0]
    links = pathway_weight.shape[0]
    units = gene_weight.shape[0]
    samples, variants = genotypes.shape
    punits = pathway_weight.shape[1] // units
    paths = head_weight.shape[0] // punits
    half = units // 2
    steps = variants // STEP
    shape = jax.ShapeDtypeStruct

    tab = pl.pallas_call(
        functools.partial(index_kernel, devs, genes, paths),
        out_shape=shape((TAB_ROWS, 128), I32),
        in_specs=[vmem()] * 3,
        out_specs=vmem(),
        scratch_shapes=[pltpu.VMEM((2 * devs, genes), F32), pltpu.VMEM((2, genes), F32)],
        compiler_params=pltpu.CompilerParams(vmem_limit_bytes=LIMIT),
        name="index",
    )(membership.T, pathway_slot.reshape(-1, 128), gene_lengths.reshape(1, -1))

    hidden = pl.pallas_call(
        functools.partial(forward_kernel, genes, units),
        out_shape=shape((genes, half, 2 * samples), BF16),
        grid=(steps,),
        in_specs=[
            smem(),
            pl.BlockSpec((samples, STEP), lambda i: (0, i)),
            pl.BlockSpec((units, STEP), lambda i: (0, i)),
        ],
        out_specs=pl.BlockSpec((genes, half, 2 * samples), lambda i: (0, 0, 0)),
        scratch_shapes=[pltpu.VMEM(((genes + 2) * units, samples), F32)],
        compiler_params=pltpu.CompilerParams(vmem_limit_bytes=LIMIT),
        name="gene_forward",
    )(tab, genotypes, gene_weight)

    link_rows = pathway_weight.reshape(links, half, 2 * punits)
    got_hidden, got_links, sibling = pl.pallas_call(
        functools.partial(send_kernel, devs),
        out_shape=(
            shape((devs + 1, CAP, half, 2 * samples), BF16),
            shape((devs + 1, CAP, half, 2 * punits), BF16),
            shape((samples, variants), BF16),
        ),
        in_specs=[smem(), vmem(), vmem(), hbm()],
        out_specs=(vmem(), vmem(), hbm()),
        scratch_shapes=[
            pltpu.VMEM((devs, CAP, half, 2 * samples), BF16),
            pltpu.VMEM((devs, HALF, half, 2 * punits), BF16),
        ]
        + [pltpu.SemaphoreType.DMA((devs,))] * 4
        + [pltpu.SemaphoreType.DMA((2,)), pltpu.SemaphoreType.DMA((2,))],
        compiler_params=pltpu.CompilerParams(
            collective_id=0, has_side_effects=True, vmem_limit_bytes=LIMIT
        ),
        name="send_links",
    )(tab, hidden, link_rows, genotypes)

    rows = (devs + 1) * CAP
    deltas, link_parts, head_part = pl.pallas_call(
        functools.partial(path_kernel, paths, punits),
        out_shape=(
            shape((rows, half, 2 * samples), BF16),
            shape((rows, half, 2 * punits), F32),
            shape((paths * punits // 128, 128), F32),
        ),
        in_specs=[smem()] + [vmem()] * 4,
        out_specs=(vmem(),) * 3,
        scratch_shapes=[
            pltpu.VMEM((MAX_GROUPS, 8 * GROUP, 2 * samples), BF16),
            pltpu.VMEM((MAX_GROUPS, 8 * GROUP, 2 * punits), BF16),
            pltpu.VMEM((paths + 1, punits, samples), F32),
            pltpu.VMEM((paths + 1, 2 * punits, 2 * samples), BF16),
        ],
        compiler_params=pltpu.CompilerParams(vmem_limit_bytes=LIMIT),
        name="pathways",
    )(
        tab,
        got_hidden.reshape(rows, half, 2 * samples),
        got_links.reshape(rows, half, 2 * punits),
        head_weight.astype(F32).reshape(-1, 128),
        cotangent.reshape(1, -1),
    )

    pad_rows = (genes + 2) * units
    own, sib, got_parts, grad_head = pl.pallas_call(
        functools.partial(return_kernel, devs, genes, units),
        out_shape=(
            shape((pad_rows, samples), BF16),
            shape((pad_rows, samples), BF16),
            shape((devs, CAP, half, 2 * punits), BF16),
            shape(head_part.shape, F32),
        ),
        in_specs=[smem()] + [vmem()] * 4,
        out_specs=(vmem(),) * 4,
        scratch_shapes=[
            pltpu.VMEM((devs, CAP, half, 2 * samples), BF16),
            pltpu.VMEM((devs, HALF, half, 2 * punits), F32),
            pltpu.VMEM((devs, HALF, half, 2 * punits), BF16),
            pltpu.VMEM(head_part.shape, F32),
            pltpu.VMEM((genes * units, samples), F32),
        ]
        + [pltpu.SemaphoreType.DMA((devs,))] * 4
        + [pltpu.SemaphoreType.DMA((8,))],
        compiler_params=pltpu.CompilerParams(
            collective_id=1, has_side_effects=True, vmem_limit_bytes=LIMIT
        ),
        name="return_links",
    )(
        tab,
        deltas.reshape(devs + 1, CAP, half, 2 * samples),
        link_parts.reshape(devs + 1, CAP, half, 2 * punits),
        head_part,
        hidden,
    )

    per = links // steps
    grad_gene, grad_pathway = pl.pallas_call(
        functools.partial(backward_kernel, units),
        out_shape=(shape((units, variants), F32), shape((links, units * punits), F32)),
        grid=(steps,),
        in_specs=[
            smem(),
            pl.BlockSpec((samples, STEP), lambda i: (0, i)),
            pl.BlockSpec((samples, STEP), lambda i: (0, i)),
            vmem(),
            vmem(),
            vmem(),
        ],
        out_specs=(
            pl.BlockSpec((units, STEP), lambda i: (0, i)),
            pl.BlockSpec((per, units * punits), lambda i: (i, 0)),
        ),
        scratch_shapes=[pltpu.VMEM((8 * per, 128), F32)],
        compiler_params=pltpu.CompilerParams(vmem_limit_bytes=LIMIT),
        name="gene_backward",
    )(tab, genotypes, sibling, own, sib, got_parts.reshape(devs * CAP, half, 2 * punits))
    return grad_gene, grad_pathway, grad_head.reshape(-1)


def solution(mesh):
    return jax.shard_map(
        on_device,
        mesh=mesh,
        in_specs=(
            P("batch", "genes"), P(None, "genes"), P("genes"), P(), P(),
            P("genes", None), P("genes"), P("batch"),
        ),
        out_specs=(P(None, "genes"), P("genes", None), P("genes")),
        check_vma=False,
    )
```

```python
import functools

import jax
import jax.numpy as jnp
from jax import lax
from jax.experimental import pallas as pl
from jax.experimental.pallas import tpu as pltpu
from jax.sharding import PartitionSpec as P

MESH = pl.DeviceIdType.MESH
F32 = jnp.float32
BF16 = jnp.bfloat16
I32 = jnp.int32

CAP = 12
HALF = CAP // 2
COLS = 256
GROUP = 32
MAX_GROUPS = 56
STRIDE = 27

ROW_SEND = 0
ROW_PERM = 12
ROW_SLOT = 26
ROW_RET = 28
ROW_OWNER = 32
ROW_ORDER = 36
ROW_FIRST = 40
ROW_ONE = 42
ROW_TWO = 44
ROW_PART = 46
TAB_ROWS = 56
CHUNK = 4096
PARTS = 3


def iota(shape, dim):
    return lax.broadcasted_iota(I32, shape, dim)


def one(mask):
    return jnp.where(mask, 1.0, 0.0).astype(BF16)


def mm(left, right):
    return jnp.dot(left, right, preferred_element_type=F32)


def mm_tn(left, right):
    return lax.dot_general(left, right, (((0,), (0,)), ((), ())), preferred_element_type=F32)


def mm_nt(left, right):
    return lax.dot_general(left, right, (((1,), (1,)), ((), ())), preferred_element_type=F32)


def to_col(row, n):
    eye = iota((n, n), 0) == iota((n, n), 1)
    return jnp.sum(jnp.where(eye, jnp.broadcast_to(row, (n, n)), 0.0), axis=1, keepdims=True)


def to_row(col, n):
    eye = iota((n, n), 0) == iota((n, n), 1)
    return jnp.sum(jnp.where(eye, jnp.broadcast_to(col, (n, n)), 0.0), axis=0, keepdims=True)


def put(tab_ref, row, values):
    width = values.shape[1]
    tab_ref[row : row + 1, :] = values[:, :128]
    tab_ref[row + 1 : row + 2, : width - 128] = values[:, 128:]


def index_kernel(
    devs, genes, paths, mem_ref, slot_ref, len_ref, link_ref, tab_ref, rows_ref,
    s_ref, own_ref, tile_ref,
):
    me = lax.axis_index("genes")
    per = genes
    table = slot_ref[...]
    halves = jnp.concatenate([table >> 5, table & 31], axis=0).astype(F32).astype(BF16)
    rows = table.shape[0]
    pair = 2 * per

    for m in range(2):
        def look(j, _, m=m):
            q = mem_ref[m : m + 1, pl.ds(pl.multiple_of(j * pair, 128), pair)]
            lane = q & 127
            which = q >> 7
            hot = one(jnp.broadcast_to(lane, (128, pair)) == iota((128, pair), 0))
            vals = mm(halves, hot)
            pick = jnp.broadcast_to(which, (rows, pair)) == iota((rows, pair), 0)
            owner = jnp.sum(jnp.where(pick, vals[:rows], 0.0), axis=0, keepdims=True)
            local = jnp.sum(jnp.where(pick, vals[rows:], 0.0), axis=0, keepdims=True)
            slot = owner * 32.0 + local
            s_ref[pl.ds(m * devs + 2 * j, 1), :] = slot[:, :per]
            s_ref[pl.ds(m * devs + 2 * j + 1, 1), :] = slot[:, per:]
            return 0

        lax.fori_loop(0, devs // 2, look, 0, unroll=4)

    tab_ref[...] = jnp.zeros((TAB_ROWS, 128), I32)
    slots = s_ref[...].astype(I32)
    mine = (slots >> 5) == me
    local = (slots & 31).astype(F32)
    upper = one(iota((per, per), 0) < iota((per, per), 1))
    before = mm(one(mine), upper)
    count = jnp.sum(jnp.where(mine, 1.0, 0.0), axis=1, keepdims=True)
    lead = jnp.concatenate([jnp.zeros((devs, 1), F32), count[:devs]], axis=0)
    rank = before + lead
    lower = one(iota((devs, devs), 1) < iota((devs, devs), 0))
    lane64 = iota((devs, 128), 1)
    carry = jnp.zeros((1, 128), F32)
    places, cells = [], []
    for r in range(CAP):
        hit = mine & (rank == float(r))
        got = jnp.sum(jnp.where(hit, local + 1.0, 0.0), axis=1, keepdims=True)
        got = got[:devs] + got[devs:]
        cell = jnp.where(got == 0.0, float(paths), got - 1.0).astype(I32)
        hot = jnp.broadcast_to(cell, (devs, 128)) == lane64
        within = mm(lower, one(hot)) + carry
        carry = carry + jnp.sum(jnp.where(hot, 1.0, 0.0), axis=0, keepdims=True)
        places.append(jnp.sum(jnp.where(hot, within, 0.0), axis=1, keepdims=True))
        cells.append(hot)
    lane1 = iota((1, 128), 1)
    groups = jnp.where(lane1 < paths, ((carry.astype(I32) + (GROUP - 1)) // GROUP).astype(F32), 0.0)
    strict = one(iota((128, 128), 0) < iota((128, 128), 1))
    start = mm(jnp.broadcast_to(groups.astype(BF16), (8, 128)), strict)[:1]
    end_col = to_col(start + groups, 128)
    ends = jnp.where(
        (jnp.broadcast_to(end_col, (128, 128)) <= iota((128, 128), 1).astype(F32))
        & (iota((128, 128), 0) < paths),
        1.0,
        0.0,
    )
    tab_ref[ROW_SLOT : ROW_SLOT + 1, :] = jnp.sum(ends, axis=0, keepdims=True).astype(I32)
    total = jnp.sum(groups, axis=1, keepdims=True)
    tab_ref[ROW_SLOT + 1 : ROW_SLOT + 2, :] = jnp.broadcast_to(total, (1, 128)).astype(I32)
    src_sum = jnp.zeros((16, 128), F32)
    rank_sum = jnp.zeros((16, 128), F32)
    seen = jnp.zeros((16, 128), F32)
    source = iota((devs, 128), 0).astype(F32).astype(BF16)
    for r in range(CAP):
        first = jnp.sum(
            jnp.where(cells[r], jnp.broadcast_to(start, (devs, 128)), 0.0), axis=1, keepdims=True
        )
        real = jnp.sum(jnp.where(cells[r] & (lane64 < paths), 1.0, 0.0), axis=1, keepdims=True)
        pos = (first * float(GROUP) + places[r]).astype(I32)
        pos = jnp.where(real > 0.0, pos, 1 << 20)
        high = one(jnp.broadcast_to(pos >> 7, (devs, 16)) == iota((devs, 16), 1))
        low = jnp.broadcast_to(pos & 127, (devs, 128)) == lane64
        src_sum = src_sum + mm_tn(high, jnp.where(low, source, jnp.zeros((), BF16)))
        found = mm_tn(high, one(low))
        rank_sum = rank_sum + found * float(r)
        seen = seen + found
    perm = jnp.where(seen > 0.0, src_sum * float(CAP) + rank_sum, float(devs * CAP))
    tab_ref[ROW_PERM : ROW_PERM + 14, :] = perm.astype(I32)[:14]

    own_ref[0:1, :] = s_ref[pl.ds(me, 1), :]
    own_ref[1:2, :] = s_ref[pl.ds(devs + me, 1), :]
    lower_g = one(iota((per, per), 1) < iota((per, per), 0))
    lane_g = iota((per, 128), 1)
    gene_col = iota((per, 128), 0).astype(F32).astype(BF16)
    carry = jnp.zeros((1, 128), F32)
    send = jnp.zeros((16, 128), F32)
    owner_rows = [own_ref[m : m + 1, :].astype(I32) >> 5 for m in range(2)]
    for m in range(2):
        owner = (to_col(own_ref[m : m + 1, :], per).astype(I32)) >> 5
        hot = jnp.broadcast_to(owner, (per, 128)) == lane_g
        within = mm(lower_g, one(hot)) + carry
        carry = carry + jnp.sum(jnp.where(hot, 1.0, 0.0), axis=0, keepdims=True)
        order = jnp.sum(jnp.where(hot, within, 0.0), axis=1, keepdims=True)
        cell = one(jnp.broadcast_to(order, (per, 16)) == iota((per, 16), 1).astype(F32))
        send = send + 2.0 * mm_tn(cell, jnp.where(hot, gene_col, jnp.zeros((), BF16)))
        if m:
            send = send + mm_tn(cell, one(hot))
        owner_row = owner_rows[m]
        order_row = to_row(order, per).astype(I32)
        put(tab_ref, ROW_RET + 2 * m, owner_row * CAP + order_row)
        put(tab_ref, ROW_OWNER + 2 * m, owner_row)
        put(tab_ref, ROW_ORDER + 2 * m, order_row)
    tab_ref[ROW_SEND : ROW_SEND + CAP, :] = send.astype(I32)[:CAP]

    lens = len_ref[...].astype(F32) - 128.0
    starts = mm(jnp.broadcast_to(lens.astype(BF16), (8, per)), upper)[:1]
    starts = starts + 128.0 * iota((1, per), 1).astype(F32)
    start_col = jnp.broadcast_to(to_col(starts, per), (per, 256))
    begin = (iota((per, 256), 1) * COLS).astype(F32)
    inside = jnp.where(start_col <= begin, 1.0, 0.0)
    put(tab_ref, ROW_FIRST, (jnp.sum(inside, axis=0, keepdims=True) - 1.0).astype(I32))
    end = float(per * COLS)
    next_one = jnp.min(jnp.where(start_col > begin, start_col, end), axis=0, keepdims=True)
    next_two = jnp.min(
        jnp.where(start_col > jnp.broadcast_to(next_one, (per, 256)), start_col, end),
        axis=0, keepdims=True,
    )
    put(tab_ref, ROW_ONE, (next_one - begin[:1]).astype(I32))
    put(tab_ref, ROW_TWO, (next_two - begin[:1]).astype(I32))
    start_col = start_col[:, :per]
    starts_i = starts.astype(I32)
    last = (starts_i + len_ref[...] - 1) >> 8
    gene_row = iota((1, per), 1)
    for j in range(PARTS):
        block = (starts_i >> 8) + j
        edge = jnp.broadcast_to((block * COLS).astype(F32), (per, per))
        under = jnp.where(start_col <= edge, 1.0, 0.0)
        lead_gene = jnp.sum(under, axis=0, keepdims=True).astype(I32) - 1
        row = block * PARTS + (gene_row - lead_gene)
        put(tab_ref, ROW_PART + 2 * j, jnp.where(block <= last, row, per * PARTS))

    def relayout(e, _):
        at = pl.multiple_of(16 * e, 16)
        rows = link_ref[pl.ds(at, 16), :].astype(F32)
        for n in range(2):
            for t in range(8):
                tile_ref[pl.ds(64 * n + t, 8, stride=8), :] = rows[
                    8 * n : 8 * n + 8, 128 * t : 128 * t + 128
                ]
        for n in range(16):
            rows_ref[at + n] = tile_ref[8 * n : 8 * n + 8, :].astype(BF16)
        return 0

    lax.fori_loop(0, link_ref.shape[0] // 16, relayout, 0)


def look_up(tab_ref, row, index):
    return tab_ref[row + (index >> 7), index & 127]


def window_of(tab_ref, block):
    return tuple(look_up(tab_ref, row, block) for row in (ROW_FIRST, ROW_ONE, ROW_TWO))


def partner(me, k):
    off = lax.rem(k * STRIDE, 64)
    x = lax.rem(me // 16 + off // 16, 4)
    z = lax.rem((me // 4) % 4 + (off // 4) % 4, 4)
    y = lax.rem(me % 4 + off % 4, 4)
    return x * 16 + z * 4 + y


def greet(devs, me, core):
    barrier = pltpu.get_barrier_semaphore()

    def hello(k, _):
        pl.semaphore_signal(
            barrier, inc=1, device_id=(partner(me, k), core), device_id_type=MESH
        )
        return 0

    lax.fori_loop(1, devs, hello, 0)
    pl.semaphore_signal(barrier, inc=1, device_id=(me, 1 - core), device_id_type=MESH)
    pl.semaphore_wait(barrier, devs)


def load_chunks(src_ref, dst_ref, sem):
    return [
        pltpu.make_async_copy(
            src_ref.at[:, pl.ds(c * CHUNK, CHUNK)], dst_ref.at[:, pl.ds(c * CHUNK, CHUNK)], sem.at[c]
        )
        for c in range(src_ref.shape[1] // CHUNK)
    ]


def send_kernel(
    devs, genes, units, tab_ref, link_ref, geno_ref, weight_ref, hid_ref, h_ref, w_ref,
    g_ref, gw_ref, part_ref, pre_ref, hs_ref, ws_ref, geno_sem, weight_sem, hsend, hrecv, wsend, wrecv,
    pair_sem,
):
    me = lax.axis_index("genes")
    core = lax.axis_index("batch")
    low = core * HALF
    loads = load_chunks(geno_ref, g_ref, geno_sem)
    weights = load_chunks(weight_ref, gw_ref, weight_sem)
    for weight, load in zip(weights, loads):
        weight.start()
        load.start()
    greet(devs, me, core)

    def w_copy(k):
        to = partner(me, k)
        return pltpu.make_async_remote_copy(
            src_ref=ws_ref.at[to], dst_ref=w_ref.at[me, pl.ds(low, HALF)],
            send_sem=wsend, recv_sem=wrecv,
            device_id=(to, core), device_id_type=MESH,
        )

    def h_copy(k):
        to = partner(me, k)
        return pltpu.make_async_remote_copy(
            src_ref=hs_ref.at[to], dst_ref=h_ref.at[me],
            send_sem=hsend, recv_sem=hrecv,
            device_id=(to, core), device_id_type=MESH,
        )

    def w_step(k, _):
        to = partner(me, k)
        for r in range(HALF):
            ws_ref[to, r] = link_ref[tab_ref[low + r, to]]
        w_copy(k).start()
        return 0

    lax.fori_loop(1, devs, w_step, 0)

    pos = iota((units, COLS), 1)
    part_ref[genes * PARTS] = jnp.zeros((units, 128), F32)
    per_chunk = CHUNK // COLS
    for c, load in enumerate(loads):
        weights[c].wait()
        load.wait()

        def block(i, _, c=c):
            for k in range(4):
                b = c * per_chunk + i * 4 + k
                _, one_end, two_end = window_of(tab_ref, b)
                cols = pl.ds(pl.multiple_of(b * COLS, COLS), COLS)
                weight = gw_ref[:, cols].astype(F32)
                not_one = pos >= one_end
                not_two = pos >= two_end
                zero = jnp.zeros_like(weight)
                basis = jnp.concatenate(
                    [
                        jnp.where(not_one, zero, weight),
                        jnp.where(not_one & jnp.logical_not(not_two), weight, zero),
                        jnp.where(not_two, weight, zero),
                    ],
                    axis=0,
                ).astype(BF16)
                got = mm_nt(basis, g_ref[:, cols])
                for w in range(PARTS):
                    part_ref[b * PARTS + w] = got[w * units : (w + 1) * units]
            return 0

        lax.fori_loop(0, per_chunk // 4, block, 0)

    def finish(i, _):
        for k in range(8):
            g = i * 8 + k
            total = part_ref[look_up(tab_ref, ROW_PART, g)]
            for j in range(1, PARTS):
                total = total + part_ref[look_up(tab_ref, ROW_PART + 2 * j, g)]
            pre_ref[pl.ds(k * units, units), :] = jnp.tanh(total)
        for k in range(8):
            even = pre_ref[pl.ds(k * units, units // 2, stride=2), :]
            odd = pre_ref[pl.ds(k * units + 1, units // 2, stride=2), :]
            hid_ref[i * 8 + k] = jnp.concatenate([even, odd], axis=1).astype(BF16)
        return 0

    lax.fori_loop(0, genes // 8, finish, 0)

    def h_step(k, _):
        to = partner(me, k)
        for r in range(CAP):
            hs_ref[to, r] = hid_ref[tab_ref[r, to] >> 1]
        h_copy(k).start()
        return 0

    lax.fori_loop(1, devs, h_step, 0)
    for r in range(CAP):
        h_ref[me, r] = hid_ref[tab_ref[r, me] >> 1]
    for r in range(HALF):
        w_ref[me, low + r] = link_ref[tab_ref[low + r, me]]
    h_ref[devs] = jnp.zeros(h_ref.shape[1:], BF16)
    w_ref[devs] = jnp.zeros(w_ref.shape[1:], BF16)

    others = pl.ds(0, devs - 1)
    pltpu.make_async_remote_copy(
        src_ref=ws_ref.at[others], dst_ref=w_ref.at[others, pl.ds(low, HALF)],
        send_sem=wsend, recv_sem=wrecv, device_id=(me, 1 - core), device_id_type=MESH,
    ).wait()
    part = w_ref.at[pl.ds(0, devs), pl.ds(low, HALF)]
    share = pltpu.make_async_remote_copy(
        src_ref=part, dst_ref=part, send_sem=pair_sem.at[0], recv_sem=pair_sem.at[1],
        device_id=(me, 1 - core), device_id_type=MESH,
    )
    share.start()

    pltpu.make_async_remote_copy(
        src_ref=hs_ref.at[others], dst_ref=h_ref.at[others],
        send_sem=hsend, recv_sem=hrecv, device_id=(me, 1 - core), device_id_type=MESH,
    ).wait()
    share.wait()


def path_kernel(
    paths, punits, tab_ref, h_ref, w_ref, head_ref, cot_ref, hd_ref, gp_ref, gh_ref,
    hs_ref, ws_ref, sum_ref, delta_ref, heads,
):
    rows = (tab_ref[ROW_SLOT + 1, 0] + 3) // 4
    sum_ref[...] = jnp.zeros_like(sum_ref)

    def up(i, _):
        for q in range(4):
            for j in range(GROUP):
                p = tab_ref[ROW_PERM + i, q * GROUP + j]
                hs_ref[4 * i + q, 8 * j : 8 * j + 8, :] = h_ref[p]
                ws_ref[4 * i + q, 8 * j : 8 * j + 8, :] = w_ref[p]
            slot = tab_ref[ROW_SLOT, 4 * i + q]
            out = mm_tn(ws_ref[4 * i + q], hs_ref[4 * i + q])
            sum_ref[slot] = sum_ref[slot] + out[:punits, :128] + out[punits:, 128:]
        return 0

    lax.fori_loop(0, rows, up, 0)

    cot = cot_ref[...]
    heads[...] = head_ref[...].astype(F32)
    lane = iota((punits, 128), 1)
    sub = iota((punits, 128), 0)

    def middle(i, _):
        row = jnp.zeros((1, 128), F32)
        head_row = heads[pl.ds(i, 1), :]
        for half in range(2):
            s = 2 * i + half
            active = jnp.tanh(sum_ref[s])
            diag = lane == sub + punits * half
            head = jnp.sum(
                jnp.where(diag, jnp.broadcast_to(head_row, (punits, 128)), 0.0),
                axis=1, keepdims=True,
            )
            grad = jnp.sum(active * cot, axis=1, keepdims=True)
            row = row + jnp.sum(
                jnp.where(diag, jnp.broadcast_to(grad, (punits, 128)), 0.0), axis=0, keepdims=True
            )
            delta = (cot * head * (1.0 - active * active)).astype(BF16)
            none = jnp.zeros_like(delta)
            delta_ref[s] = jnp.concatenate(
                [
                    jnp.concatenate([delta, none], axis=1),
                    jnp.concatenate([none, delta], axis=1),
                ],
                axis=0,
            )
        gh_ref[pl.ds(i, 1), :] = row
        return 0

    lax.fori_loop(0, paths // 2, middle, 0)
    delta_ref[paths] = jnp.zeros(delta_ref.shape[1:], BF16)

    def down(i, _):
        for q in range(4):
            block = delta_ref[tab_ref[ROW_SLOT, 4 * i + q]]
            hd = mm(ws_ref[4 * i + q], block).astype(BF16)
            gp = mm_nt(hs_ref[4 * i + q], block)
            for j in range(GROUP):
                p = tab_ref[ROW_PERM + i, q * GROUP + j]
                hd_ref[p] = hd[8 * j : 8 * j + 8]
                gp_ref[p] = gp[8 * j : 8 * j + 8]
        return 0

    lax.fori_loop(0, rows, down, 0)


def return_kernel(
    devs, genes, units, tab_ref, hd_ref, gp_ref, gh_ref, hid_ref, geno_ref,
    out_ref, path_ref, head_ref,
    g_ref, back_ref, part_ref, gs_ref, link_ref, ghs_ref, pd_ref, own_ref, sib_ref, grad_ref, rows_ref,
    geno_sem, out_sem, hsend, hrecv, gsend, grecv, pair_sem,
):
    me = lax.axis_index("genes")
    core = lax.axis_index("batch")
    low = core * HALF
    other = (1 - core) * HALF
    samples = geno_ref.shape[0]
    span = geno_ref.shape[1] // 2
    here = pl.multiple_of(core * span, span)
    there = pl.multiple_of((1 - core) * span, span)
    load = pltpu.make_async_copy(
        geno_ref.at[:, pl.ds(here, span)], g_ref.at[pl.ds(0, samples)], geno_sem
    )
    load.start()
    greet(devs, me, core)

    def pair(src, dst, n):
        return pltpu.make_async_remote_copy(
            src_ref=src, dst_ref=dst, send_sem=pair_sem.at[2 * n], recv_sem=pair_sem.at[2 * n + 1],
            device_id=(me, 1 - core), device_id_type=MESH,
        )

    def h_copy(k):
        to = partner(me, k)
        return pltpu.make_async_remote_copy(
            src_ref=hd_ref.at[pl.ds(to * CAP, CAP)], dst_ref=back_ref.at[pl.ds(me * CAP, CAP)],
            send_sem=hsend, recv_sem=hrecv,
            device_id=(to, core), device_id_type=MESH,
        )

    def g_copy(k):
        to = partner(me, k)
        return pltpu.make_async_remote_copy(
            src_ref=gs_ref.at[to], dst_ref=link_ref.at[me, pl.ds(low, HALF)],
            send_sem=gsend, recv_sem=grecv,
            device_id=(to, core), device_id_type=MESH,
        )

    def h_step(k, _):
        h_copy(k).start()
        return 0

    lax.fori_loop(1, devs, h_step, 0)
    parts = pair(gp_ref.at[pl.ds(0, devs), pl.ds(other, HALF)], part_ref, 0)
    parts.start()
    heads = pair(gh_ref, ghs_ref, 1)
    heads.start()
    geno = pair(geno_ref.at[:, pl.ds(there, span)], g_ref.at[pl.ds(samples, samples)], 2)
    geno.start()
    back_ref[pl.ds(me * CAP, CAP)] = hd_ref[pl.ds(me * CAP, CAP)]
    parts.wait()

    def g_step(k, _):
        to = partner(me, k)
        gs_ref[to] = (gp_ref[to, pl.ds(low, HALF)] + part_ref[to]).astype(BF16)
        g_copy(k).start()
        return 0

    lax.fori_loop(1, devs, g_step, 0)
    link_ref[me, pl.ds(low, HALF)] = (gp_ref[me, pl.ds(low, HALF)] + part_ref[me]).astype(BF16)
    heads.wait()
    head_ref[...] = gh_ref[...] + ghs_ref[...]
    for n in range(genes, own_ref.shape[0]):
        own_ref[n] = jnp.zeros((units, 128), BF16)
        sib_ref[n] = jnp.zeros((units, 128), BF16)

    others = pl.ds(0, devs - 1)
    pltpu.make_async_remote_copy(
        src_ref=hd_ref.at[pl.ds(0, (devs - 1) * CAP)],
        dst_ref=back_ref.at[pl.ds(0, (devs - 1) * CAP)],
        send_sem=hsend, recv_sem=hrecv, device_id=(me, 1 - core), device_id_type=MESH,
    ).wait()

    def gene(i, _):
        for k in range(4):
            g = 4 * i + k
            a = look_up(tab_ref, ROW_RET, g)
            b = look_up(tab_ref, ROW_RET + 2, g)
            both = back_ref[a].astype(F32) + back_ref[b].astype(F32)
            hid = hid_ref[g].astype(F32)
            value = both * (1.0 - hid * hid)
            pd_ref[pl.ds(k * units, units // 2, stride=2), :] = value[:, :128]
            pd_ref[pl.ds(k * units + 1, units // 2, stride=2), :] = value[:, 128:]
        for k in range(4):
            own_ref[4 * i + k] = pd_ref[pl.ds(k * units, units), :].astype(BF16)
        return 0

    quarter = genes // 4
    deltas = []
    for n in range(4):
        lax.fori_loop(n * quarter // 4, (n + 1) * quarter // 4, gene, 0)
        rows = pl.ds(n * quarter, quarter)
        delta = pair(own_ref.at[rows], sib_ref.at[rows], 4 + n)
        delta.start()
        deltas.append(delta)
    load.wait()
    geno.wait()
    for delta in deltas:
        delta.wait()

    pos = iota((units, COLS), 1)
    per_chunk = CHUNK // COLS
    stores = []
    first_block = core * (span // COLS)
    for c in range(span // CHUNK):
        def block(i, _, c=c):
            for k in range(4):
                b = c * per_chunk + i * 4 + k
                first, one_end, two_end = window_of(tab_ref, first_block + b)
                left = jnp.concatenate(
                    [
                        jnp.concatenate([ref[first + w] for w in range(PARTS)], axis=0)
                        for ref in (own_ref, sib_ref)
                    ],
                    axis=1,
                )
                cols = pl.ds(pl.multiple_of(b * COLS, COLS), COLS)
                full = mm(left, g_ref[:, cols])
                grad_ref[:, cols] = jnp.where(
                    pos >= two_end,
                    full[2 * units :],
                    jnp.where(pos >= one_end, full[units : 2 * units], full[:units]),
                )
            return 0

        lax.fori_loop(0, per_chunk // 4, block, 0)
        cols = pl.ds(pl.multiple_of(here + c * CHUNK, CHUNK), CHUNK)
        piece = grad_ref.at[:, pl.ds(c * CHUNK, CHUNK)]
        store = pltpu.make_async_copy(piece, out_ref.at[:, cols], out_sem.at[c])
        store.start()
        stores.append(store)
        store = pair(piece, out_ref.at[:, cols], 8 + c)
        store.start()
        stores.append(store)

    pltpu.make_async_remote_copy(
        src_ref=gs_ref.at[others], dst_ref=link_ref.at[others, pl.ds(low, HALF)],
        send_sem=gsend, recv_sem=grecv, device_id=(me, 1 - core), device_id_type=MESH,
    ).wait()
    part = link_ref.at[pl.ds(0, devs), pl.ds(low, HALF)]
    share = pair(part, part, 3)
    share.start()
    share.wait()

    def link_group(e, _):
        for j in range(8):
            g = e * 4 + j // 2
            owner = look_up(tab_ref, ROW_OWNER + 2 * (j % 2), g)
            order = look_up(tab_ref, ROW_ORDER + 2 * (j % 2), g)
            rows_ref[8 * j : 8 * j + 8, :] = link_ref[owner, order].astype(F32)
        for t in range(8):
            path_ref[pl.ds(pl.multiple_of(8 * e, 8), 8), 128 * t : 128 * t + 128] = rows_ref[
                pl.ds(t, 8, stride=8), :
            ]
        return 0

    lax.fori_loop(0, path_ref.shape[0] // 8, link_group, 0)
    for store in stores:
        store.wait()


def vmem():
    return pl.BlockSpec(memory_space=pltpu.VMEM)


def smem():
    return pl.BlockSpec(memory_space=pltpu.SMEM)


def hbm():
    return pl.BlockSpec(memory_space=pl.ANY)


LIMIT = 60 * 1024 * 1024


def on_device(
    genotypes, gene_weight, gene_lengths, membership, pathway_slot, pathway_weight,
    head_weight, cotangent,
):
    devs = lax.axis_size("genes")
    genes = gene_lengths.shape[0]
    links = pathway_weight.shape[0]
    units = gene_weight.shape[0]
    samples, variants = genotypes.shape
    punits = pathway_weight.shape[1] // units
    paths = head_weight.shape[0] // punits
    half = units // 2
    shape = jax.ShapeDtypeStruct

    tab, link_rows = pl.pallas_call(
        functools.partial(index_kernel, devs, genes, paths),
        out_shape=(
            shape((TAB_ROWS, 128), I32),
            shape((links, half, 2 * punits), BF16),
        ),
        in_specs=[vmem()] * 4,
        out_specs=(vmem(),) * 2,
        scratch_shapes=[
            pltpu.VMEM((2 * devs, genes), F32),
            pltpu.VMEM((2, genes), F32),
            pltpu.VMEM((128, 128), F32),
        ],
        compiler_params=pltpu.CompilerParams(vmem_limit_bytes=LIMIT),
        name="index",
    )(membership.T, pathway_slot.reshape(-1, 128), gene_lengths.reshape(1, -1), pathway_weight)

    pieces = variants // CHUNK
    hidden, got_hidden, got_links = pl.pallas_call(
        functools.partial(send_kernel, devs, genes, units),
        out_shape=(
            shape((genes, half, 2 * samples), BF16),
            shape((devs + 1, CAP, half, 2 * samples), BF16),
            shape((devs + 1, CAP, half, 2 * punits), BF16),
        ),
        in_specs=[smem(), vmem(), hbm(), hbm()],
        out_specs=(vmem(),) * 3,
        scratch_shapes=[
            pltpu.VMEM((samples, variants), BF16),
            pltpu.VMEM((units, variants), BF16),
            pltpu.VMEM((genes * PARTS + 1, units, samples), F32),
            pltpu.VMEM((8 * units, samples), F32),
            pltpu.VMEM((devs, CAP, half, 2 * samples), BF16),
            pltpu.VMEM((devs, HALF, half, 2 * punits), BF16),
        ]
        + [pltpu.SemaphoreType.DMA((pieces,))] * 2
        + [pltpu.SemaphoreType.DMA(())] * 4
        + [pltpu.SemaphoreType.DMA((2,))],
        compiler_params=pltpu.CompilerParams(
            collective_id=0, has_side_effects=True, vmem_limit_bytes=LIMIT
        ),
        name="send_links",
    )(tab, link_rows, genotypes, gene_weight)

    rows = (devs + 1) * CAP
    deltas, link_parts, head_part = pl.pallas_call(
        functools.partial(path_kernel, paths, punits),
        out_shape=(
            shape((rows, half, 2 * samples), BF16),
            shape((rows, half, 2 * punits), F32),
            shape((paths * punits // 128, 128), F32),
        ),
        in_specs=[smem()] + [vmem()] * 4,
        out_specs=(vmem(),) * 3,
        scratch_shapes=[
            pltpu.VMEM((MAX_GROUPS, 8 * GROUP, 2 * samples), BF16),
            pltpu.VMEM((MAX_GROUPS, 8 * GROUP, 2 * punits), BF16),
            pltpu.VMEM((paths + 1, punits, samples), F32),
            pltpu.VMEM((paths + 1, 2 * punits, 2 * samples), BF16),
            pltpu.VMEM((paths * punits // 128, 128), F32),
        ],
        compiler_params=pltpu.CompilerParams(vmem_limit_bytes=LIMIT),
        name="pathways",
    )(
        tab,
        got_hidden.reshape(rows, half, 2 * samples),
        got_links.reshape(rows, half, 2 * punits),
        head_weight.reshape(-1, 128),
        cotangent.reshape(1, -1),
    )

    grad_gene, grad_pathway, grad_head = pl.pallas_call(
        functools.partial(return_kernel, devs, genes, units),
        out_shape=(
            shape((units, variants), F32),
            shape((links, units * punits), F32),
            shape(head_part.shape, F32),
        ),
        in_specs=[smem()] + [vmem()] * 4 + [hbm()],
        out_specs=(hbm(), vmem(), vmem()),
        scratch_shapes=[
            pltpu.VMEM((2 * samples, variants // 2), BF16),
            pltpu.VMEM((devs * CAP, half, 2 * samples), BF16),
            pltpu.VMEM((devs, HALF, half, 2 * punits), F32),
            pltpu.VMEM((devs, HALF, half, 2 * punits), BF16),
            pltpu.VMEM((devs, CAP, half, 2 * punits), BF16),
            pltpu.VMEM(head_part.shape, F32),
            pltpu.VMEM((4 * units, samples), F32),
            pltpu.VMEM((genes + 2, units, samples), BF16),
            pltpu.VMEM((genes + 2, units, samples), BF16),
            pltpu.VMEM((units, variants // 2), F32),
            pltpu.VMEM((8 * half, 2 * punits), F32),
        ]
        + [pltpu.SemaphoreType.DMA(()), pltpu.SemaphoreType.DMA((pieces // 2,))]
        + [pltpu.SemaphoreType.DMA(())] * 4
        + [pltpu.SemaphoreType.DMA((16 + pieces,))],
        compiler_params=pltpu.CompilerParams(
            collective_id=1, has_side_effects=True, vmem_limit_bytes=LIMIT
        ),
        name="return_links",
    )(
        tab,
        deltas,
        link_parts.reshape(devs + 1, CAP, half, 2 * punits),
        head_part,
        hidden,
        genotypes,
    )
    return grad_gene, grad_pathway, grad_head.reshape(-1)


def solution(mesh):
    return jax.shard_map(
        on_device,
        mesh=mesh,
        in_specs=(
            P("batch", "genes"), P(None, "genes"), P("genes"), P(), P(),
            P("genes", None), P("genes"), P("batch"),
        ),
        out_specs=(P(None, "genes"), P("genes", None), P("genes")),
        check_vma=False,
    )
```

```python
import functools

import jax
import jax.numpy as jnp
from jax import lax
from jax.experimental import pallas as pl
from jax.experimental.pallas import tpu as pltpu
from jax.sharding import PartitionSpec as P

MESH = pl.DeviceIdType.MESH
F32 = jnp.float32
BF16 = jnp.bfloat16
I32 = jnp.int32

CAP = 12
HALF = CAP // 2
COLS = 256
GROUP = 16
GROUPS = 80
STRIDE = 27

ROW_SEND = 0
ROW_PERM = 12
ROW_SLOT = 22
ROW_LAST = 23
ROW_RET = 28
ROW_LINK = 32
ROW_FIRST = 40
ROW_ONE = 42
ROW_TWO = 44
ROW_PART = 46
ROW_POS = 52
ROW_PERM_W = 64
TAB_ROWS = 80
CHUNK = 4096
PARTS = 3


def iota(shape, dim):
    return lax.broadcasted_iota(I32, shape, dim)


def one(mask):
    return jnp.where(mask, 1.0, 0.0).astype(BF16)


def mm(left, right):
    return jnp.dot(left, right, preferred_element_type=F32)


def mm_tn(left, right):
    return lax.dot_general(left, right, (((0,), (0,)), ((), ())), preferred_element_type=F32)


def mm_nt(left, right):
    return lax.dot_general(left, right, (((1,), (1,)), ((), ())), preferred_element_type=F32)


def to_col(row, n):
    eye = iota((n, n), 0) == iota((n, n), 1)
    return jnp.sum(jnp.where(eye, jnp.broadcast_to(row, (n, n)), 0.0), axis=1, keepdims=True)


def to_row(col, n):
    eye = iota((n, n), 0) == iota((n, n), 1)
    return jnp.sum(jnp.where(eye, jnp.broadcast_to(col, (n, n)), 0.0), axis=0, keepdims=True)


def put(tab_ref, row, values):
    width = values.shape[1]
    tab_ref[row : row + 1, :] = values[:, :128]
    tab_ref[row + 1 : row + 2, : width - 128] = values[:, 128:]


def index_kernel(
    devs, genes, paths, mem_ref, slot_ref, len_ref, link_ref, tab_ref, rows_ref,
    s_ref, own_ref, tile_ref,
):
    me = lax.axis_index("genes")
    per = genes
    table = slot_ref[...]
    halves = jnp.concatenate([table >> 5, table & 31], axis=0).astype(F32).astype(BF16)
    rows = table.shape[0]
    pair = 2 * per

    for m in range(2):
        def look(j, _, m=m):
            q = mem_ref[m : m + 1, pl.ds(pl.multiple_of(j * pair, 128), pair)]
            lane = q & 127
            which = q >> 7
            hot = one(jnp.broadcast_to(lane, (128, pair)) == iota((128, pair), 0))
            vals = mm(halves, hot)
            pick = jnp.broadcast_to(which, (rows, pair)) == iota((rows, pair), 0)
            owner = jnp.sum(jnp.where(pick, vals[:rows], 0.0), axis=0, keepdims=True)
            local = jnp.sum(jnp.where(pick, vals[rows:], 0.0), axis=0, keepdims=True)
            slot = owner * 32.0 + local
            s_ref[pl.ds(m * devs + 2 * j, 1), :] = slot[:, :per]
            s_ref[pl.ds(m * devs + 2 * j + 1, 1), :] = slot[:, per:]
            return 0

        lax.fori_loop(0, devs // 2, look, 0, unroll=4)

    tab_ref[...] = jnp.zeros((TAB_ROWS, 128), I32)
    slots = s_ref[...].astype(I32)
    mine = (slots >> 5) == me
    local = (slots & 31).astype(F32)
    upper = one(iota((per, per), 0) < iota((per, per), 1))
    before = mm(one(mine), upper)
    count = jnp.sum(jnp.where(mine, 1.0, 0.0), axis=1, keepdims=True)
    lead = jnp.concatenate([jnp.zeros((devs, 1), F32), count[:devs]], axis=0)
    rank = before + lead
    lower = one(iota((devs, devs), 1) < iota((devs, devs), 0))
    lane64 = iota((devs, 128), 1)
    carry = jnp.zeros((1, 128), F32)
    places, cells = [], []
    for r in range(CAP):
        hit = mine & (rank == float(r))
        got = jnp.sum(jnp.where(hit, local + 1.0, 0.0), axis=1, keepdims=True)
        got = got[:devs] + got[devs:]
        cell = jnp.where(got == 0.0, float(paths), got - 1.0).astype(I32)
        hot = jnp.broadcast_to(cell, (devs, 128)) == lane64
        within = mm(lower, one(hot)) + carry
        carry = carry + jnp.sum(jnp.where(hot, 1.0, 0.0), axis=0, keepdims=True)
        places.append(jnp.sum(jnp.where(hot, within, 0.0), axis=1, keepdims=True))
        cells.append(hot)
    lane1 = iota((1, 128), 1)
    groups = jnp.where(lane1 < paths, ((carry.astype(I32) + (GROUP - 1)) // GROUP).astype(F32), 0.0)
    strict = one(iota((128, 128), 0) < iota((128, 128), 1))
    start = mm(jnp.broadcast_to(groups.astype(BF16), (8, 128)), strict)[:1]
    end_col = to_col(start + groups, 128)
    ends = jnp.where(
        (jnp.broadcast_to(end_col, (128, 128)) <= iota((128, 128), 1).astype(F32))
        & (iota((128, 128), 0) < paths),
        1.0,
        0.0,
    )
    tab_ref[ROW_SLOT : ROW_SLOT + 1, :] = jnp.sum(ends, axis=0, keepdims=True).astype(I32)
    final = jnp.where(groups > 0.0, start + groups - 1.0, float(GROUPS))
    tab_ref[ROW_LAST : ROW_LAST + 1, :] = final.astype(I32)
    src_sum = jnp.zeros((16, 128), F32)
    rank_sum = jnp.zeros((16, 128), F32)
    link_sum = jnp.zeros((16, 128), F32)
    seen = jnp.zeros((16, 128), F32)
    source = iota((devs, 128), 0).astype(F32).astype(BF16)
    for r in range(CAP):
        first = jnp.sum(
            jnp.where(cells[r], jnp.broadcast_to(start, (devs, 128)), 0.0), axis=1, keepdims=True
        )
        real = jnp.sum(jnp.where(cells[r] & (lane64 < paths), 1.0, 0.0), axis=1, keepdims=True)
        pos = first * float(GROUP) + places[r]
        tab_ref[ROW_POS + r : ROW_POS + r + 1, :devs] = to_row(
            jnp.where(real > 0.0, pos, 0.0), devs
        ).astype(I32)
        pos = jnp.where(real > 0.0, pos.astype(I32), 1 << 20)
        high = one(jnp.broadcast_to(pos >> 7, (devs, 16)) == iota((devs, 16), 1))
        low = jnp.broadcast_to(pos & 127, (devs, 128)) == lane64
        src_sum = src_sum + mm_tn(high, jnp.where(low, source, jnp.zeros((), BF16)))
        found = mm_tn(high, one(low))
        rank_sum = rank_sum + found * float(r)
        link_sum = link_sum + found * float(r if r < HALF else r + (devs - 1) * HALF)
        seen = seen + found
    perm = jnp.where(seen > 0.0, src_sum * float(CAP) + rank_sum, float(devs * CAP))
    tab_ref[ROW_PERM : ROW_PERM + 10, :] = perm.astype(I32)[:10]
    perm = jnp.where(seen > 0.0, src_sum * float(HALF) + link_sum, float(devs * CAP))
    tab_ref[ROW_PERM_W : ROW_PERM_W + 10, :] = perm.astype(I32)[:10]

    own_ref[0:1, :] = s_ref[pl.ds(me, 1), :]
    own_ref[1:2, :] = s_ref[pl.ds(devs + me, 1), :]
    lower_g = one(iota((per, per), 1) < iota((per, per), 0))
    lane_g = iota((per, 128), 1)
    gene_col = iota((per, 128), 0).astype(F32).astype(BF16)
    carry = jnp.zeros((1, 128), F32)
    send = jnp.zeros((16, 128), F32)
    owner_rows = [own_ref[m : m + 1, :].astype(I32) >> 5 for m in range(2)]
    for m in range(2):
        owner = (to_col(own_ref[m : m + 1, :], per).astype(I32)) >> 5
        hot = jnp.broadcast_to(owner, (per, 128)) == lane_g
        within = mm(lower_g, one(hot)) + carry
        carry = carry + jnp.sum(jnp.where(hot, 1.0, 0.0), axis=0, keepdims=True)
        order = jnp.sum(jnp.where(hot, within, 0.0), axis=1, keepdims=True)
        cell = one(jnp.broadcast_to(order, (per, 16)) == iota((per, 16), 1).astype(F32))
        send = send + 2.0 * mm_tn(cell, jnp.where(hot, gene_col, jnp.zeros((), BF16)))
        if m:
            send = send + mm_tn(cell, one(hot))
        owner_row = owner_rows[m]
        order_row = to_row(order, per).astype(I32)
        put(tab_ref, ROW_RET + 2 * m, owner_row * CAP + order_row)
        link_row = owner_row * HALF + order_row
        link_row = jnp.where(order_row < HALF, link_row, link_row + (devs - 1) * HALF)
        put(tab_ref, ROW_LINK + 2 * m, link_row)
    tab_ref[ROW_SEND : ROW_SEND + CAP, :] = send.astype(I32)[:CAP]

    lens = len_ref[...].astype(F32) - 128.0
    starts = mm(jnp.broadcast_to(lens.astype(BF16), (8, per)), upper)[:1]
    starts = starts + 128.0 * iota((1, per), 1).astype(F32)
    start_col = jnp.broadcast_to(to_col(starts, per), (per, 256))
    begin = (iota((per, 256), 1) * COLS).astype(F32)
    inside = jnp.where(start_col <= begin, 1.0, 0.0)
    put(tab_ref, ROW_FIRST, (jnp.sum(inside, axis=0, keepdims=True) - 1.0).astype(I32))
    end = float(per * COLS)
    next_one = jnp.min(jnp.where(start_col > begin, start_col, end), axis=0, keepdims=True)
    next_two = jnp.min(
        jnp.where(start_col > jnp.broadcast_to(next_one, (per, 256)), start_col, end),
        axis=0, keepdims=True,
    )
    put(tab_ref, ROW_ONE, (next_one - begin[:1]).astype(I32))
    put(tab_ref, ROW_TWO, (next_two - begin[:1]).astype(I32))
    start_col = start_col[:, :per]
    starts_i = starts.astype(I32)
    last = (starts_i + len_ref[...] - 1) >> 8
    gene_row = iota((1, per), 1)
    for j in range(PARTS):
        block = (starts_i >> 8) + j
        edge = jnp.broadcast_to((block * COLS).astype(F32), (per, per))
        under = jnp.where(start_col <= edge, 1.0, 0.0)
        lead_gene = jnp.sum(under, axis=0, keepdims=True).astype(I32) - 1
        row = block * PARTS + (gene_row - lead_gene)
        put(tab_ref, ROW_PART + 2 * j, jnp.where(block <= last, row, per * PARTS))

    def relayout(e, _):
        at = pl.multiple_of(16 * e, 16)
        rows = link_ref[pl.ds(at, 16), :].astype(F32)
        for n in range(2):
            for t in range(8):
                tile_ref[pl.ds(64 * n + t, 8, stride=8), :] = rows[
                    8 * n : 8 * n + 8, 128 * t : 128 * t + 128
                ]
        for n in range(16):
            rows_ref[at + n] = tile_ref[8 * n : 8 * n + 8, :].astype(BF16)
        return 0

    lax.fori_loop(0, link_ref.shape[0] // 16, relayout, 0)


def look_up(tab_ref, row, index):
    return tab_ref[row + (index >> 7), index & 127]


def window_of(tab_ref, block):
    return tuple(look_up(tab_ref, row, block) for row in (ROW_FIRST, ROW_ONE, ROW_TWO))


def partner(me, k):
    off = lax.rem(k * STRIDE, 64)
    x = lax.rem(me // 16 + off // 16, 4)
    z = lax.rem((me // 4) % 4 + (off // 4) % 4, 4)
    y = lax.rem(me % 4 + off % 4, 4)
    return x * 16 + z * 4 + y


def greet(devs, me, core):
    barrier = pltpu.get_barrier_semaphore()

    def hello(k, _):
        pl.semaphore_signal(
            barrier, inc=1, device_id=(partner(me, k), core), device_id_type=MESH
        )
        return 0

    lax.fori_loop(1, devs, hello, 0)
    pl.semaphore_signal(barrier, inc=1, device_id=(me, 1 - core), device_id_type=MESH)
    pl.semaphore_wait(barrier, devs)


def load_chunks(src_ref, dst_ref, sem):
    return [
        pltpu.make_async_copy(
            src_ref.at[:, pl.ds(c * CHUNK, CHUNK)], dst_ref.at[:, pl.ds(c * CHUNK, CHUNK)], sem.at[c]
        )
        for c in range(src_ref.shape[1] // CHUNK)
    ]


def main_kernel(
    devs, genes, units, paths, punits,
    tab_ref, link_ref, head_ref, cot_ref, geno_ref, weight_ref,
    out_ref, path_ref, gh_ref,
    g_ref, gsib_ref, gw_ref, hid_ref, h_ref, w_ref, hs_ref, ws_ref, he_ref, wl_ref, gp_ref,
    hd_ref, delta_ref, heads_ref, own_gh, sib_gh, give_ref, take_ref, back_ref, lrow_ref,
    own_ref, sib_ref, grad_ref, tile_ref,
    geno_sem, weight_sem, out_sem, hsend, hrecv, wsend, wrecv, dsend, drecv, lsend, lrecv, pair_sem,
):
    me = lax.axis_index("genes")
    core = lax.axis_index("batch")
    low = core * HALF
    high = (1 - core) * HALF
    samples = geno_ref.shape[0]
    half = units // 2
    tiles = punits // 8
    span = geno_ref.shape[1] // 2
    here = pl.multiple_of(core * span, span)
    there = pl.multiple_of((1 - core) * span, span)
    flat = pl.ds(0, (devs - 1) * CAP)
    flat_half = pl.ds(0, (devs - 1) * HALF)
    mine = core * (devs * HALF)
    loads = load_chunks(geno_ref, g_ref, geno_sem)
    weights = load_chunks(weight_ref, gw_ref, weight_sem)
    for weight, load in zip(weights, loads):
        weight.start()
        load.start()
    greet(devs, me, core)

    def send(src, dst, send_sem, recv_sem, to):
        return pltpu.make_async_remote_copy(
            src_ref=src, dst_ref=dst, send_sem=send_sem, recv_sem=recv_sem,
            device_id=(to, core), device_id_type=MESH,
        )

    def pair(src, dst, n):
        return pltpu.make_async_remote_copy(
            src_ref=src, dst_ref=dst, send_sem=pair_sem.at[2 * n], recv_sem=pair_sem.at[2 * n + 1],
            device_id=(me, 1 - core), device_id_type=MESH,
        )

    def w_step(k, _):
        to = partner(me, k)
        for r in range(HALF):
            ws_ref[to * HALF + r] = link_ref[tab_ref[low + r, to]]
        send(
            ws_ref.at[pl.ds(to * HALF, HALF)], w_ref.at[pl.ds(mine + me * HALF, HALF)],
            wsend, wrecv, to,
        ).start()
        return 0

    lax.fori_loop(1, devs, w_step, 0)

    pos = iota((units, COLS), 1)
    for n in range(2):
        gp_ref[2 * genes * PARTS + n] = jnp.zeros((8, 128), F32)
    per_chunk = CHUNK // COLS
    for c, load in enumerate(loads):
        weights[c].wait()
        load.wait()

        def block(i, _, c=c):
            for k in range(4):
                b = c * per_chunk + i * 4 + k
                _, one_end, two_end = window_of(tab_ref, b)
                cols = pl.ds(pl.multiple_of(b * COLS, COLS), COLS)
                weight = gw_ref[:, cols].astype(F32)
                not_one = pos >= one_end
                not_two = pos >= two_end
                zero = jnp.zeros_like(weight)
                basis = jnp.concatenate(
                    [
                        jnp.where(not_one, zero, weight),
                        jnp.where(not_one & jnp.logical_not(not_two), weight, zero),
                        jnp.where(not_two, weight, zero),
                    ],
                    axis=0,
                ).astype(BF16)
                got = mm_nt(basis, g_ref[:, cols])
                for w in range(2 * PARTS):
                    gp_ref[b * 2 * PARTS + w] = got[8 * w : 8 * w + 8]
            return 0

        lax.fori_loop(0, per_chunk // 4, block, 0)
    geno = pair(g_ref.at[:, pl.ds(there, span)], gsib_ref, 0)
    geno.start()

    def finish(i, _):
        for k in range(8):
            at = [2 * look_up(tab_ref, ROW_PART + 2 * j, i * 8 + k) for j in range(PARTS)]
            for n in range(2):
                total = gp_ref[at[0] + n] + gp_ref[at[1] + n] + gp_ref[at[2] + n]
                tile_ref[k * units + 8 * n : k * units + 8 * n + 8, :] = jnp.tanh(total)
        for k in range(8):
            even = tile_ref[pl.ds(k * units, half, stride=2), :]
            odd = tile_ref[pl.ds(k * units + 1, half, stride=2), :]
            hid_ref[i * 8 + k] = jnp.concatenate([even, odd], axis=1).astype(BF16)
        return 0

    lax.fori_loop(0, genes // 8, finish, 0)

    def h_step(k, _):
        to = partner(me, k)
        for r in range(CAP):
            hs_ref[to * CAP + r] = hid_ref[tab_ref[r, to] >> 1]
        send(
            hs_ref.at[pl.ds(to * CAP, CAP)], h_ref.at[pl.ds(me * CAP, CAP)], hsend, hrecv, to
        ).start()
        return 0

    lax.fori_loop(1, devs, h_step, 0)
    for r in range(CAP):
        h_ref[me * CAP + r] = hid_ref[tab_ref[r, me] >> 1]
    for r in range(HALF):
        w_ref[mine + me * HALF + r] = link_ref[tab_ref[low + r, me]]
    h_ref[devs * CAP] = jnp.zeros(h_ref.shape[1:], BF16)
    w_ref[devs * CAP] = jnp.zeros(w_ref.shape[1:], BF16)
    send(ws_ref.at[flat_half], w_ref.at[flat_half], wsend, wrecv, me).wait()
    part = w_ref.at[pl.ds(mine, devs * HALF)]
    share = pair(part, part, 8 + span // CHUNK)
    share.start()
    share.wait()

    def gather_w(i, _):
        for q in range(128 // GROUP):
            for j in range(GROUP):
                wl_ref[i * (128 // GROUP) + q, 8 * j : 8 * j + 8, :] = w_ref[
                    tab_ref[ROW_PERM_W + i, q * GROUP + j]
                ]
        return 0

    lax.fori_loop(0, GROUPS * GROUP // 128, gather_w, 0)
    heads_ref[...] = head_ref[...].astype(F32)
    for t in range(tiles):
        gp_ref[GROUPS * tiles + t] = jnp.zeros((8, 128), F32)
    delta_ref[paths] = jnp.zeros((punits, 128), BF16)
    for n in range(genes, own_ref.shape[0]):
        own_ref[n] = jnp.zeros((units, 128), BF16)
        sib_ref[n] = jnp.zeros((units, 128), BF16)
    send(hs_ref.at[flat], h_ref.at[flat], hsend, hrecv, me).wait()

    def up(i, carry):
        for q in range(128 // GROUP):
            c = i * (128 // GROUP) + q
            for j in range(GROUP):
                p = tab_ref[ROW_PERM + i, q * GROUP + j]
                he_ref[c, 8 * j : 8 * j + 8, :] = h_ref[p]
            out = mm_tn(wl_ref[c], he_ref[c])
            out = out[:punits, :128] + out[punits:, 128:]
            slot = tab_ref[ROW_SLOT, c]
            prev, total = carry
            total = out + jnp.where(slot == prev, total, jnp.zeros_like(total))
            for t in range(tiles):
                gp_ref[c * tiles + t] = total[8 * t : 8 * t + 8]
            carry = (slot, total)
        return carry

    lax.fori_loop(
        0, GROUPS * GROUP // 128, up, (jnp.full((), -1, I32), jnp.zeros((punits, 128), F32))
    )

    cot = cot_ref[...]
    lane = iota((punits, 128), 1)
    sub = iota((punits, 128), 0)

    def middle(i, _):
        row = jnp.zeros((1, 128), F32)
        head_row = heads_ref[pl.ds(i, 1), :]
        for n in range(2):
            s = 2 * i + n
            at = tab_ref[ROW_LAST, s] * tiles
            active = jnp.tanh(
                jnp.concatenate([gp_ref[at + t] for t in range(tiles)], axis=0)
            )
            diag = lane == sub + punits * n
            head = jnp.sum(
                jnp.where(diag, jnp.broadcast_to(head_row, (punits, 128)), 0.0),
                axis=1, keepdims=True,
            )
            grad = jnp.sum(active * cot, axis=1, keepdims=True)
            row = row + jnp.sum(
                jnp.where(diag, jnp.broadcast_to(grad, (punits, 128)), 0.0), axis=0, keepdims=True
            )
            delta_ref[s] = (cot * head * (1.0 - active * active)).astype(BF16)
        own_gh[pl.ds(i, 1), :] = row
        return 0

    lax.fori_loop(0, paths // 2, middle, 0)

    def down(i, _):
        for q in range(4):
            c = i * 4 + q
            delta = delta_ref[tab_ref[ROW_SLOT, c]]
            none = jnp.zeros_like(delta)
            wide = jnp.concatenate(
                [
                    jnp.concatenate([delta, none], axis=1),
                    jnp.concatenate([none, delta], axis=1),
                ],
                axis=0,
            )
            gp = mm_nt(he_ref[c], wide)
            hd = mm(wl_ref[c], wide).astype(BF16)
            for j in range(GROUP):
                gp_ref[c * GROUP + j] = gp[8 * j : 8 * j + 8]
                hd_ref[c * GROUP + j] = hd[8 * j : 8 * j + 8]
        return 0

    lax.fori_loop(0, GROUPS // 4, down, 0)

    def d_step(k, _):
        to = partner(me, k)
        for r in range(CAP):
            hs_ref[to * CAP + r] = hd_ref[tab_ref[ROW_POS + r, to]]
        send(
            hs_ref.at[pl.ds(to * CAP, CAP)], back_ref.at[pl.ds(me * CAP, CAP)], dsend, drecv, to
        ).start()
        return 0

    lax.fori_loop(1, devs, d_step, 0)

    def give_step(i, _):
        for r in range(HALF):
            give_ref[i * HALF + r] = gp_ref[tab_ref[ROW_POS + high + r, i]]
        return 0

    lax.fori_loop(0, devs, give_step, 0)
    parts = pair(give_ref, take_ref, 1)
    parts.start()
    swap = pair(own_gh, sib_gh, 2)
    swap.start()
    for r in range(CAP):
        back_ref[me * CAP + r] = hd_ref[tab_ref[ROW_POS + r, me]]
    parts.wait()

    def l_step(k, _):
        to = partner(me, k)
        for r in range(HALF):
            ws_ref[to * HALF + r] = (
                gp_ref[tab_ref[ROW_POS + low + r, to]] + take_ref[to * HALF + r]
            ).astype(BF16)
        send(
            ws_ref.at[pl.ds(to * HALF, HALF)], lrow_ref.at[pl.ds(mine + me * HALF, HALF)],
            lsend, lrecv, to,
        ).start()
        return 0

    lax.fori_loop(1, devs, l_step, 0)
    for r in range(HALF):
        lrow_ref[mine + me * HALF + r] = (
            gp_ref[tab_ref[ROW_POS + low + r, me]] + take_ref[me * HALF + r]
        ).astype(BF16)
    swap.wait()
    gh_ref[...] = own_gh[...] + sib_gh[...]
    send(hs_ref.at[flat], back_ref.at[flat], dsend, drecv, me).wait()

    def gene(i, _):
        for k in range(4):
            g = 4 * i + k
            a = look_up(tab_ref, ROW_RET, g)
            b = look_up(tab_ref, ROW_RET + 2, g)
            both = back_ref[a].astype(F32) + back_ref[b].astype(F32)
            hid = hid_ref[g].astype(F32)
            value = both * (1.0 - hid * hid)
            tile_ref[pl.ds(k * units, half, stride=2), :] = value[:, :128]
            tile_ref[pl.ds(k * units + 1, half, stride=2), :] = value[:, 128:]
        for k in range(4):
            own_ref[4 * i + k] = tile_ref[k * units : (k + 1) * units, :].astype(BF16)
        return 0

    quarter = genes // 4
    deltas = []
    for n in range(4):
        lax.fori_loop(n * quarter // 4, (n + 1) * quarter // 4, gene, 0)
        rows = pl.ds(n * quarter, quarter)
        delta = pair(own_ref.at[rows], sib_ref.at[rows], 4 + n)
        delta.start()
        deltas.append(delta)
    geno.wait()
    for delta in deltas:
        delta.wait()

    stores = []
    first_block = core * (span // COLS)
    for c in range(span // CHUNK):
        def block(i, _, c=c):
            for k in range(4):
                b = c * per_chunk + i * 4 + k
                first, one_end, two_end = window_of(tab_ref, first_block + b)
                left = jnp.concatenate(
                    [
                        jnp.concatenate([ref[first + w] for w in range(PARTS)], axis=0)
                        for ref in (own_ref, sib_ref)
                    ],
                    axis=1,
                )
                cols = pl.ds(pl.multiple_of(b * COLS, COLS), COLS)
                whole = pl.ds(pl.multiple_of(here + b * COLS, COLS), COLS)
                right = jnp.concatenate([g_ref[:, whole], gsib_ref[:, cols]], axis=0)
                full = mm(left, right)
                grad_ref[:, cols] = jnp.where(
                    pos >= two_end,
                    full[2 * units :],
                    jnp.where(pos >= one_end, full[units : 2 * units], full[:units]),
                )
            return 0

        lax.fori_loop(0, per_chunk // 4, block, 0)
        cols = pl.ds(pl.multiple_of(here + c * CHUNK, CHUNK), CHUNK)
        piece = grad_ref.at[:, pl.ds(c * CHUNK, CHUNK)]
        store = pltpu.make_async_copy(piece, out_ref.at[:, cols], out_sem.at[c])
        store.start()
        stores.append(store)
        store = pair(piece, out_ref.at[:, cols], 8 + c)
        store.start()
        stores.append(store)

    send(ws_ref.at[flat_half], lrow_ref.at[flat_half], lsend, lrecv, me).wait()
    part = lrow_ref.at[pl.ds(mine, devs * HALF)]
    share = pair(part, part, 3)
    share.start()
    share.wait()

    def link_group(e, _):
        for j in range(8):
            g = e * 4 + j // 2
            at = look_up(tab_ref, ROW_LINK + 2 * (j % 2), g)
            tile_ref[8 * j : 8 * j + 8, :] = lrow_ref[at].astype(F32)
        for t in range(8):
            path_ref[pl.ds(pl.multiple_of(8 * e, 8), 8), 128 * t : 128 * t + 128] = tile_ref[
                pl.ds(t, 8, stride=8), :
            ]
        return 0

    lax.fori_loop(0, path_ref.shape[0] // 8, link_group, 0)
    for store in stores:
        store.wait()


def vmem():
    return pl.BlockSpec(memory_space=pltpu.VMEM)


def smem():
    return pl.BlockSpec(memory_space=pltpu.SMEM)


def hbm():
    return pl.BlockSpec(memory_space=pl.ANY)


LIMIT = 60 * 1024 * 1024


def on_device(
    genotypes, gene_weight, gene_lengths, membership, pathway_slot, pathway_weight,
    head_weight, cotangent,
):
    devs = lax.axis_size("genes")
    genes = gene_lengths.shape[0]
    links = pathway_weight.shape[0]
    units = gene_weight.shape[0]
    samples, variants = genotypes.shape
    punits = pathway_weight.shape[1] // units
    paths = head_weight.shape[0] // punits
    half = units // 2
    shape = jax.ShapeDtypeStruct

    tab, link_rows = pl.pallas_call(
        functools.partial(index_kernel, devs, genes, paths),
        out_shape=(
            shape((TAB_ROWS, 128), I32),
            shape((links, half, 2 * punits), BF16),
        ),
        in_specs=[vmem()] * 4,
        out_specs=(vmem(),) * 2,
        scratch_shapes=[
            pltpu.VMEM((2 * devs, genes), F32),
            pltpu.VMEM((2, genes), F32),
            pltpu.VMEM((128, 128), F32),
        ],
        compiler_params=pltpu.CompilerParams(vmem_limit_bytes=LIMIT),
        name="index",
    )(membership.T, pathway_slot.reshape(-1, 128), gene_lengths.reshape(1, -1), pathway_weight)

    pieces = variants // CHUNK
    sem = pltpu.SemaphoreType.DMA
    heads = (paths * punits // 128, 128)
    tile = lambda n, width, kind: pltpu.VMEM((n, half, width), kind)
    grad_gene, grad_pathway, grad_head = pl.pallas_call(
        functools.partial(main_kernel, devs, genes, units, paths, punits),
        out_shape=(
            shape((units, variants), F32),
            shape((links, units * punits), F32),
            shape(heads, F32),
        ),
        in_specs=[smem()] + [vmem()] * 3 + [hbm()] * 2,
        out_specs=(hbm(), vmem(), vmem()),
        scratch_shapes=[
            pltpu.VMEM((samples, variants), BF16),
            pltpu.VMEM((samples, variants // 2), BF16),
            pltpu.VMEM((units, variants), BF16),
            tile(genes, 2 * samples, BF16),
            tile(devs * CAP + 1, 2 * samples, BF16),
            tile(devs * CAP + 1, 2 * punits, BF16),
            tile(devs * CAP, 2 * samples, BF16),
            tile(devs * HALF, 2 * punits, BF16),
            pltpu.VMEM((GROUPS, half * GROUP, 2 * samples), BF16),
            pltpu.VMEM((GROUPS, half * GROUP, 2 * punits), BF16),
            tile(GROUPS * GROUP, 2 * punits, F32),
            tile(GROUPS * GROUP, 2 * samples, BF16),
            pltpu.VMEM((paths + 1, punits, samples), BF16),
            pltpu.VMEM(heads, F32),
            pltpu.VMEM(heads, F32),
            pltpu.VMEM(heads, F32),
            tile(devs * HALF, 2 * punits, F32),
            tile(devs * HALF, 2 * punits, F32),
            tile(devs * CAP, 2 * samples, BF16),
            tile(devs * CAP, 2 * punits, BF16),
            pltpu.VMEM((genes + 2, units, samples), BF16),
            pltpu.VMEM((genes + 2, units, samples), BF16),
            pltpu.VMEM((units, variants // 2), F32),
            pltpu.VMEM((8 * units, samples), F32),
        ]
        + [sem((pieces,))] * 2
        + [sem((pieces // 2,))]
        + [sem(())] * 8
        + [sem((18 + pieces,))],
        compiler_params=pltpu.CompilerParams(
            collective_id=0, has_side_effects=True, vmem_limit_bytes=66_000_000
        ),
        name="main",
    )(
        tab,
        link_rows,
        head_weight.reshape(-1, 128),
        cotangent.reshape(1, -1),
        genotypes,
        gene_weight,
    )
    return grad_gene, grad_pathway, grad_head.reshape(-1)


def solution(mesh):
    return jax.shard_map(
        on_device,
        mesh=mesh,
        in_specs=(
            P("batch", "genes"), P(None, "genes"), P("genes"), P(), P(),
            P("genes", None), P("genes"), P("batch"),
        ),
        out_specs=(P(None, "genes"), P("genes", None), P("genes")),
        check_vma=False,
    )
```

```python
import functools

import jax
import jax.numpy as jnp
from jax import lax
from jax.experimental import pallas as pl
from jax.experimental.pallas import tpu as pltpu
from jax.sharding import PartitionSpec as P

MESH = pl.DeviceIdType.MESH
F32 = jnp.float32
BF16 = jnp.bfloat16
I32 = jnp.int32

CAP = 12
HALF = CAP // 2
COLS = 256
GROUP = 16
GROUPS = 80
STRIDE = 27

ROW_SEND = 0
ROW_PERM = 12
ROW_SLOT = 22
ROW_LAST = 23
ROW_RET = 28
ROW_LINK = 32
ROW_FIRST = 40
ROW_ONE = 42
ROW_TWO = 44
ROW_PART = 46
ROW_POS = 52
ROW_PERM_W = 64
TAB_ROWS = 80
CHUNK = 4096
PARTS = 3


def iota(shape, dim):
    return lax.broadcasted_iota(I32, shape, dim)


def one(mask):
    return jnp.where(mask, 1.0, 0.0).astype(BF16)


def mm(left, right):
    return jnp.dot(left, right, preferred_element_type=F32)


def mm_tn(left, right):
    return lax.dot_general(left, right, (((0,), (0,)), ((), ())), preferred_element_type=F32)


def mm_nt(left, right):
    return lax.dot_general(left, right, (((1,), (1,)), ((), ())), preferred_element_type=F32)


def to_col(row, n):
    eye = iota((n, n), 0) == iota((n, n), 1)
    return jnp.sum(jnp.where(eye, jnp.broadcast_to(row, (n, n)), 0.0), axis=1, keepdims=True)


def to_row(col, n):
    eye = iota((n, n), 0) == iota((n, n), 1)
    return jnp.sum(jnp.where(eye, jnp.broadcast_to(col, (n, n)), 0.0), axis=0, keepdims=True)


def put(tab_ref, row, values):
    width = values.shape[1]
    tab_ref[row : row + 1, :] = values[:, :128]
    tab_ref[row + 1 : row + 2, : width - 128] = values[:, 128:]


def index_kernel(
    devs, genes, paths, mem_ref, slot_ref, len_ref, link_ref, tab_ref, rows_ref,
    s_ref, own_ref, tile_ref,
):
    me = lax.axis_index("genes")
    per = genes
    table = slot_ref[...]
    halves = jnp.concatenate([table >> 5, table & 31], axis=0).astype(F32).astype(BF16)
    rows = table.shape[0]
    pair = 2 * per

    for m in range(2):
        def look(j, _, m=m):
            q = mem_ref[m : m + 1, pl.ds(pl.multiple_of(j * pair, 128), pair)]
            lane = q & 127
            which = q >> 7
            hot = one(jnp.broadcast_to(lane, (128, pair)) == iota((128, pair), 0))
            vals = mm(halves, hot)
            pick = jnp.broadcast_to(which, (rows, pair)) == iota((rows, pair), 0)
            owner = jnp.sum(jnp.where(pick, vals[:rows], 0.0), axis=0, keepdims=True)
            local = jnp.sum(jnp.where(pick, vals[rows:], 0.0), axis=0, keepdims=True)
            slot = owner * 32.0 + local
            s_ref[pl.ds(m * devs + 2 * j, 1), :] = slot[:, :per]
            s_ref[pl.ds(m * devs + 2 * j + 1, 1), :] = slot[:, per:]
            return 0

        lax.fori_loop(0, devs // 2, look, 0, unroll=4)

    tab_ref[...] = jnp.zeros((TAB_ROWS, 128), I32)
    slots = s_ref[...].astype(I32)
    mine = (slots >> 5) == me
    local = (slots & 31).astype(F32)
    upper = one(iota((per, per), 0) < iota((per, per), 1))
    before = mm(one(mine), upper)
    count = jnp.sum(jnp.where(mine, 1.0, 0.0), axis=1, keepdims=True)
    lead = jnp.concatenate([jnp.zeros((devs, 1), F32), count[:devs]], axis=0)
    rank = before + lead
    lower = one(iota((devs, devs), 1) < iota((devs, devs), 0))
    lane64 = iota((devs, 128), 1)
    carry = jnp.zeros((1, 128), F32)
    places, cells = [], []
    for r in range(CAP):
        hit = mine & (rank == float(r))
        got = jnp.sum(jnp.where(hit, local + 1.0, 0.0), axis=1, keepdims=True)
        got = got[:devs] + got[devs:]
        cell = jnp.where(got == 0.0, float(paths), got - 1.0).astype(I32)
        hot = jnp.broadcast_to(cell, (devs, 128)) == lane64
        within = mm(lower, one(hot)) + carry
        carry = carry + jnp.sum(jnp.where(hot, 1.0, 0.0), axis=0, keepdims=True)
        places.append(jnp.sum(jnp.where(hot, within, 0.0), axis=1, keepdims=True))
        cells.append(hot)
    lane1 = iota((1, 128), 1)
    groups = jnp.where(lane1 < paths, ((carry.astype(I32) + (GROUP - 1)) // GROUP).astype(F32), 0.0)
    strict = one(iota((128, 128), 0) < iota((128, 128), 1))
    start = mm(jnp.broadcast_to(groups.astype(BF16), (8, 128)), strict)[:1]
    end_col = to_col(start + groups, 128)
    ends = jnp.where(
        (jnp.broadcast_to(end_col, (128, 128)) <= iota((128, 128), 1).astype(F32))
        & (iota((128, 128), 0) < paths),
        1.0,
        0.0,
    )
    tab_ref[ROW_SLOT : ROW_SLOT + 1, :] = jnp.sum(ends, axis=0, keepdims=True).astype(I32)
    final = jnp.where(groups > 0.0, start + groups - 1.0, float(GROUPS))
    tab_ref[ROW_LAST : ROW_LAST + 1, :] = final.astype(I32)
    src_sum = jnp.zeros((16, 128), F32)
    rank_sum = jnp.zeros((16, 128), F32)
    link_sum = jnp.zeros((16, 128), F32)
    seen = jnp.zeros((16, 128), F32)
    source = iota((devs, 128), 0).astype(F32).astype(BF16)
    for r in range(CAP):
        first = jnp.sum(
            jnp.where(cells[r], jnp.broadcast_to(start, (devs, 128)), 0.0), axis=1, keepdims=True
        )
        real = jnp.sum(jnp.where(cells[r] & (lane64 < paths), 1.0, 0.0), axis=1, keepdims=True)
        pos = first * float(GROUP) + places[r]
        tab_ref[ROW_POS + r : ROW_POS + r + 1, :devs] = to_row(
            jnp.where(real > 0.0, pos, 0.0), devs
        ).astype(I32)
        pos = jnp.where(real > 0.0, pos.astype(I32), 1 << 20)
        high = one(jnp.broadcast_to(pos >> 7, (devs, 16)) == iota((devs, 16), 1))
        low = jnp.broadcast_to(pos & 127, (devs, 128)) == lane64
        src_sum = src_sum + mm_tn(high, jnp.where(low, source, jnp.zeros((), BF16)))
        found = mm_tn(high, one(low))
        rank_sum = rank_sum + found * float(r)
        link_sum = link_sum + found * float(r if r < HALF else r + (devs - 1) * HALF)
        seen = seen + found
    perm = jnp.where(seen > 0.0, src_sum * float(CAP) + rank_sum, float(devs * CAP))
    tab_ref[ROW_PERM : ROW_PERM + 10, :] = perm.astype(I32)[:10]
    perm = jnp.where(seen > 0.0, src_sum * float(HALF) + link_sum, float(devs * CAP))
    tab_ref[ROW_PERM_W : ROW_PERM_W + 10, :] = perm.astype(I32)[:10]

    own_ref[0:1, :] = s_ref[pl.ds(me, 1), :]
    own_ref[1:2, :] = s_ref[pl.ds(devs + me, 1), :]
    lower_g = one(iota((per, per), 1) < iota((per, per), 0))
    lane_g = iota((per, 128), 1)
    gene_col = iota((per, 128), 0).astype(F32).astype(BF16)
    carry = jnp.zeros((1, 128), F32)
    send = jnp.zeros((16, 128), F32)
    owner_rows = [own_ref[m : m + 1, :].astype(I32) >> 5 for m in range(2)]
    for m in range(2):
        owner = (to_col(own_ref[m : m + 1, :], per).astype(I32)) >> 5
        hot = jnp.broadcast_to(owner, (per, 128)) == lane_g
        within = mm(lower_g, one(hot)) + carry
        carry = carry + jnp.sum(jnp.where(hot, 1.0, 0.0), axis=0, keepdims=True)
        order = jnp.sum(jnp.where(hot, within, 0.0), axis=1, keepdims=True)
        cell = one(jnp.broadcast_to(order, (per, 16)) == iota((per, 16), 1).astype(F32))
        send = send + 2.0 * mm_tn(cell, jnp.where(hot, gene_col, jnp.zeros((), BF16)))
        if m:
            send = send + mm_tn(cell, one(hot))
        owner_row = owner_rows[m]
        order_row = to_row(order, per).astype(I32)
        put(tab_ref, ROW_RET + 2 * m, owner_row * CAP + order_row)
        link_row = owner_row * HALF + order_row
        link_row = jnp.where(order_row < HALF, link_row, link_row + (devs - 1) * HALF)
        put(tab_ref, ROW_LINK + 2 * m, link_row)
    tab_ref[ROW_SEND : ROW_SEND + CAP, :] = send.astype(I32)[:CAP]

    lens = len_ref[...].astype(F32) - 128.0
    starts = mm(jnp.broadcast_to(lens.astype(BF16), (8, per)), upper)[:1]
    starts = starts + 128.0 * iota((1, per), 1).astype(F32)
    start_col = jnp.broadcast_to(to_col(starts, per), (per, 256))
    begin = (iota((per, 256), 1) * COLS).astype(F32)
    inside = jnp.where(start_col <= begin, 1.0, 0.0)
    put(tab_ref, ROW_FIRST, (jnp.sum(inside, axis=0, keepdims=True) - 1.0).astype(I32))
    end = float(per * COLS)
    next_one = jnp.min(jnp.where(start_col > begin, start_col, end), axis=0, keepdims=True)
    next_two = jnp.min(
        jnp.where(start_col > jnp.broadcast_to(next_one, (per, 256)), start_col, end),
        axis=0, keepdims=True,
    )
    put(tab_ref, ROW_ONE, (next_one - begin[:1]).astype(I32))
    put(tab_ref, ROW_TWO, (next_two - begin[:1]).astype(I32))
    start_col = start_col[:, :per]
    starts_i = starts.astype(I32)
    last = (starts_i + len_ref[...] - 1) >> 8
    gene_row = iota((1, per), 1)
    for j in range(PARTS):
        block = (starts_i >> 8) + j
        edge = jnp.broadcast_to((block * COLS).astype(F32), (per, per))
        under = jnp.where(start_col <= edge, 1.0, 0.0)
        lead_gene = jnp.sum(under, axis=0, keepdims=True).astype(I32) - 1
        row = block * PARTS + (gene_row - lead_gene)
        put(tab_ref, ROW_PART + 2 * j, jnp.where(block <= last, row, per * PARTS))

    def relayout(e, _):
        at = pl.multiple_of(16 * e, 16)
        rows = link_ref[pl.ds(at, 16), :].astype(F32)
        for n in range(2):
            for t in range(8):
                tile_ref[pl.ds(64 * n + t, 8, stride=8), :] = rows[
                    8 * n : 8 * n + 8, 128 * t : 128 * t + 128
                ]
        for n in range(16):
            rows_ref[at + n] = tile_ref[8 * n : 8 * n + 8, :].astype(BF16)
        return 0

    lax.fori_loop(0, link_ref.shape[0] // 16, relayout, 0)


def look_up(tab_ref, row, index):
    return tab_ref[row + (index >> 7), index & 127]


def window_of(tab_ref, block):
    return tuple(look_up(tab_ref, row, block) for row in (ROW_FIRST, ROW_ONE, ROW_TWO))


def partner(me, k):
    off = lax.rem(k * STRIDE, 64)
    x = lax.rem(me // 16 + off // 16, 4)
    z = lax.rem((me // 4) % 4 + (off // 4) % 4, 4)
    y = lax.rem(me % 4 + off % 4, 4)
    return x * 16 + z * 4 + y


def greet(devs, me, core):
    barrier = pltpu.get_barrier_semaphore()

    def hello(k, _):
        pl.semaphore_signal(
            barrier, inc=1, device_id=(partner(me, k), core), device_id_type=MESH
        )
        return 0

    lax.fori_loop(1, devs, hello, 0, unroll=3)
    pl.semaphore_signal(barrier, inc=1, device_id=(me, 1 - core), device_id_type=MESH)
    pl.semaphore_wait(barrier, devs)


def load_chunks(src_ref, dst_ref, sem):
    return [
        pltpu.make_async_copy(
            src_ref.at[:, pl.ds(c * CHUNK, CHUNK)], dst_ref.at[:, pl.ds(c * CHUNK, CHUNK)], sem.at[c]
        )
        for c in range(src_ref.shape[1] // CHUNK)
    ]


def main_kernel(
    devs, genes, units, paths, punits,
    tab_ref, link_ref, head_ref, cot_ref, geno_ref, weight_ref,
    out_ref, lrow_ref, gh_ref,
    g_ref, gsib_ref, gw_ref, hid_ref, h_ref, w_ref, hs_ref, ws_ref, he_ref, wl_ref, gp_ref,
    hd_ref, delta_ref, heads_ref, own_gh, sib_gh, give_ref, take_ref, back_ref,
    own_ref, sib_ref, grad_ref, tile_ref,
    geno_sem, weight_sem, out_sem, hsend, hrecv, wsend, wrecv, dsend, drecv, lsend, lrecv, pair_sem,
):
    me = lax.axis_index("genes")
    core = lax.axis_index("batch")
    low = core * HALF
    high = (1 - core) * HALF
    samples = geno_ref.shape[0]
    half = units // 2
    tiles = punits // 8
    span = geno_ref.shape[1] // 2
    here = pl.multiple_of(core * span, span)
    there = pl.multiple_of((1 - core) * span, span)
    flat = pl.ds(0, (devs - 1) * CAP)
    flat_half = pl.ds(0, (devs - 1) * HALF)
    mine = core * (devs * HALF)
    loads = load_chunks(geno_ref, g_ref, geno_sem)
    weights = load_chunks(weight_ref, gw_ref, weight_sem)
    for weight, load in zip(weights, loads):
        weight.start()
        load.start()
    greet(devs, me, core)

    def send(src, dst, send_sem, recv_sem, to):
        return pltpu.make_async_remote_copy(
            src_ref=src, dst_ref=dst, send_sem=send_sem, recv_sem=recv_sem,
            device_id=(to, core), device_id_type=MESH,
        )

    def pair(src, dst, n):
        return pltpu.make_async_remote_copy(
            src_ref=src, dst_ref=dst, send_sem=pair_sem.at[2 * n], recv_sem=pair_sem.at[2 * n + 1],
            device_id=(me, 1 - core), device_id_type=MESH,
        )

    def w_step(k, _):
        to = partner(me, k)
        for r in range(HALF):
            ws_ref[to * HALF + r] = link_ref[tab_ref[low + r, to]]
        send(
            ws_ref.at[pl.ds(to * HALF, HALF)], w_ref.at[pl.ds(mine + me * HALF, HALF)],
            wsend, wrecv, to,
        ).start()
        return 0

    lax.fori_loop(1, devs, w_step, 0, unroll=3)

    pos = iota((units, COLS), 1)
    for n in range(2):
        gp_ref[2 * genes * PARTS + n] = jnp.zeros((8, 128), F32)
    per_chunk = CHUNK // COLS
    for c, load in enumerate(loads):
        weights[c].wait()
        load.wait()

        def block(i, _, c=c):
            for k in range(4):
                b = c * per_chunk + i * 4 + k
                _, one_end, two_end = window_of(tab_ref, b)
                cols = pl.ds(pl.multiple_of(b * COLS, COLS), COLS)
                weight = gw_ref[:, cols].astype(F32)
                not_one = pos >= one_end
                not_two = pos >= two_end
                zero = jnp.zeros_like(weight)
                basis = jnp.concatenate(
                    [
                        jnp.where(not_one, zero, weight),
                        jnp.where(not_one & jnp.logical_not(not_two), weight, zero),
                        jnp.where(not_two, weight, zero),
                    ],
                    axis=0,
                ).astype(BF16)
                got = mm_nt(basis, g_ref[:, cols])
                for w in range(2 * PARTS):
                    gp_ref[b * 2 * PARTS + w] = got[8 * w : 8 * w + 8]
            return 0

        lax.fori_loop(0, per_chunk // 4, block, 0)
    geno = pair(g_ref.at[:, pl.ds(there, span)], gsib_ref, 0)
    geno.start()

    def finish(i, _):
        for k in range(8):
            at = [2 * look_up(tab_ref, ROW_PART + 2 * j, i * 8 + k) for j in range(PARTS)]
            for n in range(2):
                total = gp_ref[at[0] + n] + gp_ref[at[1] + n] + gp_ref[at[2] + n]
                tile_ref[k * units + 8 * n : k * units + 8 * n + 8, :] = jnp.tanh(total)
        for k in range(8):
            even = tile_ref[pl.ds(k * units, half, stride=2), :]
            odd = tile_ref[pl.ds(k * units + 1, half, stride=2), :]
            hid_ref[i * 8 + k] = jnp.concatenate([even, odd], axis=1).astype(BF16)
        return 0

    lax.fori_loop(0, genes // 8, finish, 0)

    def h_step(k, _):
        to = partner(me, k)
        for r in range(CAP):
            hs_ref[to * CAP + r] = hid_ref[tab_ref[r, to] >> 1]
        send(
            hs_ref.at[pl.ds(to * CAP, CAP)], h_ref.at[pl.ds(me * CAP, CAP)], hsend, hrecv, to
        ).start()
        return 0

    lax.fori_loop(1, devs, h_step, 0)
    for r in range(CAP):
        h_ref[me * CAP + r] = hid_ref[tab_ref[r, me] >> 1]
    for r in range(HALF):
        w_ref[mine + me * HALF + r] = link_ref[tab_ref[low + r, me]]
    h_ref[devs * CAP] = jnp.zeros(h_ref.shape[1:], BF16)
    w_ref[devs * CAP] = jnp.zeros(w_ref.shape[1:], BF16)
    send(ws_ref.at[flat_half], w_ref.at[flat_half], wsend, wrecv, me).wait()
    part = w_ref.at[pl.ds(mine, devs * HALF)]
    share = pair(part, part, 8 + span // CHUNK)
    share.start()
    share.wait()

    def gather_w(i, _):
        for q in range(128 // GROUP):
            for j in range(GROUP):
                wl_ref[i * (128 // GROUP) + q, 8 * j : 8 * j + 8, :] = w_ref[
                    tab_ref[ROW_PERM_W + i, q * GROUP + j]
                ]
        return 0

    lax.fori_loop(0, GROUPS * GROUP // 128, gather_w, 0)
    heads_ref[...] = head_ref[...].astype(F32)
    for t in range(tiles):
        gp_ref[GROUPS * tiles + t] = jnp.zeros((8, 128), F32)
    delta_ref[paths] = jnp.zeros((punits, 128), BF16)
    for n in range(genes, own_ref.shape[0]):
        own_ref[n] = jnp.zeros((units, 128), BF16)
        sib_ref[n] = jnp.zeros((units, 128), BF16)
    send(hs_ref.at[flat], h_ref.at[flat], hsend, hrecv, me).wait()

    def up(i, carry):
        for q in range(128 // GROUP):
            c = i * (128 // GROUP) + q
            for j in range(GROUP):
                p = tab_ref[ROW_PERM + i, q * GROUP + j]
                he_ref[c, 8 * j : 8 * j + 8, :] = h_ref[p]
            out = mm_tn(wl_ref[c], he_ref[c])
            out = out[:punits, :128] + out[punits:, 128:]
            slot = tab_ref[ROW_SLOT, c]
            prev, total = carry
            total = out + jnp.where(slot == prev, total, jnp.zeros_like(total))
            for t in range(tiles):
                gp_ref[c * tiles + t] = total[8 * t : 8 * t + 8]
            carry = (slot, total)
        return carry

    lax.fori_loop(
        0, GROUPS * GROUP // 128, up, (jnp.full((), -1, I32), jnp.zeros((punits, 128), F32))
    )

    cot = cot_ref[...]
    lane = iota((punits, 128), 1)
    sub = iota((punits, 128), 0)

    def middle(i, _):
        row = jnp.zeros((1, 128), F32)
        head_row = heads_ref[pl.ds(i, 1), :]
        for n in range(2):
            s = 2 * i + n
            at = tab_ref[ROW_LAST, s] * tiles
            active = jnp.tanh(
                jnp.concatenate([gp_ref[at + t] for t in range(tiles)], axis=0)
            )
            diag = lane == sub + punits * n
            head = jnp.sum(
                jnp.where(diag, jnp.broadcast_to(head_row, (punits, 128)), 0.0),
                axis=1, keepdims=True,
            )
            grad = jnp.sum(active * cot, axis=1, keepdims=True)
            row = row + jnp.sum(
                jnp.where(diag, jnp.broadcast_to(grad, (punits, 128)), 0.0), axis=0, keepdims=True
            )
            delta_ref[s] = (cot * head * (1.0 - active * active)).astype(BF16)
        own_gh[pl.ds(i, 1), :] = row
        return 0

    lax.fori_loop(0, paths // 2, middle, 0)

    def wide_of(c):
        delta = delta_ref[tab_ref[ROW_SLOT, c]]
        none = jnp.zeros_like(delta)
        return jnp.concatenate(
            [
                jnp.concatenate([delta, none], axis=1),
                jnp.concatenate([none, delta], axis=1),
            ],
            axis=0,
        )

    def down(i, _):
        for q in range(4):
            c = i * 4 + q
            hd = mm(wl_ref[c], wide_of(c)).astype(BF16)
            for j in range(GROUP):
                hd_ref[c * GROUP + j] = hd[8 * j : 8 * j + 8]
        return 0

    lax.fori_loop(0, GROUPS // 4, down, 0)

    def d_step(k, _):
        to = partner(me, k)
        for r in range(CAP):
            hs_ref[to * CAP + r] = hd_ref[tab_ref[ROW_POS + r, to]]
        send(
            hs_ref.at[pl.ds(to * CAP, CAP)], back_ref.at[pl.ds(me * CAP, CAP)], dsend, drecv, to
        ).start()
        return 0

    lax.fori_loop(1, devs, d_step, 0)

    def down_links(i, _):
        for q in range(4):
            c = i * 4 + q
            gp = mm_nt(he_ref[c], wide_of(c))
            for j in range(GROUP):
                gp_ref[c * GROUP + j] = gp[8 * j : 8 * j + 8]
        return 0

    lax.fori_loop(0, GROUPS // 4, down_links, 0)

    def give_step(i, _):
        for r in range(HALF):
            give_ref[i * HALF + r] = gp_ref[tab_ref[ROW_POS + high + r, i]]
        return 0

    lax.fori_loop(0, devs, give_step, 0)
    parts = pair(give_ref, take_ref, 1)
    parts.start()
    swap = pair(own_gh, sib_gh, 2)
    swap.start()
    for r in range(CAP):
        back_ref[me * CAP + r] = hd_ref[tab_ref[ROW_POS + r, me]]
    parts.wait()

    def l_step(k, _):
        to = partner(me, k)
        for r in range(HALF):
            ws_ref[to * HALF + r] = (
                gp_ref[tab_ref[ROW_POS + low + r, to]] + take_ref[to * HALF + r]
            ).astype(BF16)
        send(
            ws_ref.at[pl.ds(to * HALF, HALF)], lrow_ref.at[pl.ds(mine + me * HALF, HALF)],
            lsend, lrecv, to,
        ).start()
        return 0

    lax.fori_loop(1, devs, l_step, 0)
    for r in range(HALF):
        lrow_ref[mine + me * HALF + r] = (
            gp_ref[tab_ref[ROW_POS + low + r, me]] + take_ref[me * HALF + r]
        ).astype(BF16)
    swap.wait()
    gh_ref[...] = own_gh[...] + sib_gh[...]
    send(hs_ref.at[flat], back_ref.at[flat], dsend, drecv, me).wait()

    def gene(i, _):
        for k in range(4):
            g = 4 * i + k
            a = look_up(tab_ref, ROW_RET, g)
            b = look_up(tab_ref, ROW_RET + 2, g)
            both = back_ref[a].astype(F32) + back_ref[b].astype(F32)
            hid = hid_ref[g].astype(F32)
            value = both * (1.0 - hid * hid)
            tile_ref[pl.ds(k * units, half, stride=2), :] = value[:, :128]
            tile_ref[pl.ds(k * units + 1, half, stride=2), :] = value[:, 128:]
        for k in range(4):
            own_ref[4 * i + k] = tile_ref[k * units : (k + 1) * units, :].astype(BF16)
        return 0

    quarter = genes // 4
    deltas = []
    for n in range(4):
        lax.fori_loop(n * quarter // 4, (n + 1) * quarter // 4, gene, 0)
        rows = pl.ds(n * quarter, quarter)
        delta = pair(own_ref.at[rows], sib_ref.at[rows], 4 + n)
        delta.start()
        deltas.append(delta)
    geno.wait()
    for delta in deltas:
        delta.wait()

    stores = []
    first_block = core * (span // COLS)
    for c in range(span // CHUNK):
        def block(i, _, c=c):
            for k in range(4):
                b = c * per_chunk + i * 4 + k
                first, one_end, two_end = window_of(tab_ref, first_block + b)
                left = jnp.concatenate(
                    [
                        jnp.concatenate([ref[first + w] for w in range(PARTS)], axis=0)
                        for ref in (own_ref, sib_ref)
                    ],
                    axis=1,
                )
                cols = pl.ds(pl.multiple_of(b * COLS, COLS), COLS)
                whole = pl.ds(pl.multiple_of(here + b * COLS, COLS), COLS)
                right = jnp.concatenate([g_ref[:, whole], gsib_ref[:, cols]], axis=0)
                full = mm(left, right)
                grad_ref[:, cols] = jnp.where(
                    pos >= two_end,
                    full[2 * units :],
                    jnp.where(pos >= one_end, full[units : 2 * units], full[:units]),
                )
            return 0

        lax.fori_loop(0, per_chunk // 4, block, 0)
        cols = pl.ds(pl.multiple_of(here + c * CHUNK, CHUNK), CHUNK)
        piece = grad_ref.at[:, pl.ds(c * CHUNK, CHUNK)]
        store = pltpu.make_async_copy(piece, out_ref.at[:, cols], out_sem.at[c])
        store.start()
        stores.append(store)
        store = pair(piece, out_ref.at[:, cols], 8 + c)
        store.start()
        stores.append(store)

    send(ws_ref.at[flat_half], lrow_ref.at[flat_half], lsend, lrecv, me).wait()
    part = lrow_ref.at[pl.ds(mine, devs * HALF)]
    share = pair(part, part, 3)
    share.start()
    share.wait()

    for store in stores:
        store.wait()


def final_kernel(
    tab_ref, link_hbm, grad_ref, head_ref, out_ref, path_ref, gh_ref,
    link_ref, piece_ref, rows_ref, tile_ref, link_sem, in_sem, out_sem, path_sem,
):
    pieces = in_sem.shape[0]
    links = path_ref.shape[0]
    per = links // pieces
    fetch = pltpu.make_async_copy(link_hbm, link_ref, link_sem)
    fetch.start()
    reads = load_chunks(grad_ref, piece_ref, in_sem)
    for read in reads:
        read.start()
    gh_ref[...] = head_ref[...]
    fetch.wait()
    writes = []
    for c in range(pieces):

        for n in range(per // 8):
            for j in range(8):
                e = c * per // 8 + n
                at = look_up(tab_ref, ROW_LINK + 2 * (j % 2), e * 4 + j // 2)
                tile_ref[64 * n + 8 * j : 64 * n + 8 * j + 8, :] = link_ref[at].astype(F32)
        for n in range(per // 8):
            e = c * per // 8 + n
            for t in range(8):
                rows_ref[8 * e : 8 * e + 8, 128 * t : 128 * t + 128] = tile_ref[
                    pl.ds(64 * n + t, 8, stride=8), :
                ]
        rows = pl.ds(c * per, per)
        writes.append(pltpu.make_async_copy(rows_ref.at[rows], path_ref.at[rows], path_sem.at[c]))
        writes[-1].start()
        reads[c].wait()
        cols = pl.ds(c * CHUNK, CHUNK)
        writes.append(
            pltpu.make_async_copy(piece_ref.at[:, cols], out_ref.at[:, cols], out_sem.at[c])
        )
        writes[-1].start()
    for write in writes:
        write.wait()


def vmem():
    return pl.BlockSpec(memory_space=pltpu.VMEM)


def smem():
    return pl.BlockSpec(memory_space=pltpu.SMEM)


def hbm():
    return pl.BlockSpec(memory_space=pl.ANY)


LIMIT = 60 * 1024 * 1024


def on_device(
    genotypes, gene_weight, gene_lengths, membership, pathway_slot, pathway_weight,
    head_weight, cotangent,
):
    devs = lax.axis_size("genes")
    genes = gene_lengths.shape[0]
    links = pathway_weight.shape[0]
    units = gene_weight.shape[0]
    samples, variants = genotypes.shape
    punits = pathway_weight.shape[1] // units
    paths = head_weight.shape[0] // punits
    half = units // 2
    shape = jax.ShapeDtypeStruct

    tab, link_rows = pl.pallas_call(
        functools.partial(index_kernel, devs, genes, paths),
        out_shape=(
            shape((TAB_ROWS, 128), I32),
            shape((links, half, 2 * punits), BF16),
        ),
        in_specs=[vmem()] * 4,
        out_specs=(vmem(),) * 2,
        scratch_shapes=[
            pltpu.VMEM((2 * devs, genes), F32),
            pltpu.VMEM((2, genes), F32),
            pltpu.VMEM((128, 128), F32),
        ],
        compiler_params=pltpu.CompilerParams(vmem_limit_bytes=LIMIT),
        name="index",
    )(membership.T, pathway_slot.reshape(-1, 128), gene_lengths.reshape(1, -1), pathway_weight)

    pieces = variants // CHUNK
    sem = pltpu.SemaphoreType.DMA
    heads = (paths * punits // 128, 128)
    tile = lambda n, width, kind: pltpu.VMEM((n, half, width), kind)
    grad_parts, link_parts, head_parts = pl.pallas_call(
        functools.partial(main_kernel, devs, genes, units, paths, punits),
        out_shape=(
            shape((units, variants), F32),
            shape((devs * CAP, half, 2 * punits), BF16),
            shape(heads, F32),
        ),
        in_specs=[smem()] + [vmem()] * 3 + [hbm()] * 2,
        out_specs=(hbm(), vmem(), vmem()),
        scratch_shapes=[
            pltpu.VMEM((samples, variants), BF16),
            pltpu.VMEM((samples, variants // 2), BF16),
            pltpu.VMEM((units, variants), BF16),
            tile(genes, 2 * samples, BF16),
            tile(devs * CAP + 1, 2 * samples, BF16),
            tile(devs * CAP + 1, 2 * punits, BF16),
            tile(devs * CAP, 2 * samples, BF16),
            tile(devs * HALF, 2 * punits, BF16),
            pltpu.VMEM((GROUPS, half * GROUP, 2 * samples), BF16),
            pltpu.VMEM((GROUPS, half * GROUP, 2 * punits), BF16),
            tile(GROUPS * GROUP, 2 * punits, F32),
            tile(GROUPS * GROUP, 2 * samples, BF16),
            pltpu.VMEM((paths + 1, punits, samples), BF16),
            pltpu.VMEM(heads, F32),
            pltpu.VMEM(heads, F32),
            pltpu.VMEM(heads, F32),
            tile(devs * HALF, 2 * punits, F32),
            tile(devs * HALF, 2 * punits, F32),
            tile(devs * CAP, 2 * samples, BF16),
            pltpu.VMEM((genes + 2, units, samples), BF16),
            pltpu.VMEM((genes + 2, units, samples), BF16),
            pltpu.VMEM((units, variants // 2), F32),
            pltpu.VMEM((8 * units, samples), F32),
        ]
        + [sem((pieces,))] * 2
        + [sem((pieces // 2,))]
        + [sem(())] * 8
        + [sem((18 + pieces,))],
        compiler_params=pltpu.CompilerParams(
            collective_id=0, has_side_effects=True, vmem_limit_bytes=66_000_000
        ),
        name="main",
    )(
        tab,
        link_rows,
        head_weight.reshape(-1, 128),
        cotangent.reshape(1, -1),
        genotypes,
        gene_weight,
    )
    grad_gene, grad_pathway, grad_head = pl.pallas_call(
        final_kernel,
        out_shape=(
            shape((units, variants), F32),
            shape((links, units * punits), F32),
            shape(heads, F32),
        ),
        in_specs=[smem(), hbm(), hbm(), vmem()],
        out_specs=(hbm(), hbm(), vmem()),
        scratch_shapes=[
            pltpu.VMEM(link_parts.shape, BF16),
            pltpu.VMEM((units, variants), F32),
            pltpu.VMEM((links, units * punits), F32),
            pltpu.VMEM((links // pieces * half, 2 * punits), F32),
            sem(()),
            sem((pieces,)),
            sem((pieces,)),
            sem((pieces,)),
        ],
        compiler_params=pltpu.CompilerParams(vmem_limit_bytes=LIMIT),
        name="final",
    )(tab, link_parts, grad_parts, head_parts)
    return grad_gene, grad_pathway, grad_head.reshape(-1)


def solution(mesh):
    return jax.shard_map(
        on_device,
        mesh=mesh,
        in_specs=(
            P("batch", "genes"), P(None, "genes"), P("genes"), P(), P(),
            P("genes", None), P("genes"), P("batch"),
        ),
        out_specs=(P(None, "genes"), P("genes", None), P("genes")),
        check_vma=False,
    )
```

```python
import functools

import jax
import jax.numpy as jnp
from jax import lax
from jax.experimental import pallas as pl
from jax.experimental.pallas import tpu as pltpu
from jax.sharding import PartitionSpec as P

MESH = pl.DeviceIdType.MESH
F32 = jnp.float32
BF16 = jnp.bfloat16
I32 = jnp.int32

CAP = 12
HALF = CAP // 2
COLS = 256
GROUP = 16
GROUPS = 80
STRIDE = 27

ROW_SEND = 0
ROW_PERM = 12
ROW_SLOT = 22
ROW_LAST = 23
ROW_RET = 28
ROW_LINK = 32
ROW_FIRST = 40
ROW_ONE = 42
ROW_TWO = 44
ROW_PART = 46
ROW_POS = 52
ROW_PERM_W = 64
TAB_ROWS = 80
CHUNK = 4096
PARTS = 3


def iota(shape, dim):
    return lax.broadcasted_iota(I32, shape, dim)


def one(mask):
    return jnp.where(mask, 1.0, 0.0).astype(BF16)


def mm(left, right):
    return jnp.dot(left, right, preferred_element_type=F32)


def mm_tn(left, right):
    return lax.dot_general(left, right, (((0,), (0,)), ((), ())), preferred_element_type=F32)


def mm_nt(left, right):
    return lax.dot_general(left, right, (((1,), (1,)), ((), ())), preferred_element_type=F32)


def to_col(row, n):
    eye = iota((n, n), 0) == iota((n, n), 1)
    return jnp.sum(jnp.where(eye, jnp.broadcast_to(row, (n, n)), 0.0), axis=1, keepdims=True)


def to_row(col, n):
    eye = iota((n, n), 0) == iota((n, n), 1)
    return jnp.sum(jnp.where(eye, jnp.broadcast_to(col, (n, n)), 0.0), axis=0, keepdims=True)


def put(tab_ref, row, values):
    width = values.shape[1]
    tab_ref[row : row + 1, :] = values[:, :128]
    tab_ref[row + 1 : row + 2, : width - 128] = values[:, 128:]


def index_kernel(
    devs, genes, paths, mem_ref, slot_ref, len_ref, link_ref, tab_ref, rows_ref,
    s_ref, own_ref, tile_ref,
):
    me = lax.axis_index("genes")
    per = genes
    table = slot_ref[...]
    halves = jnp.concatenate([table >> 5, table & 31], axis=0).astype(F32).astype(BF16)
    rows = table.shape[0]
    pair = 2 * per

    for m in range(2):
        def look(j, _, m=m):
            q = mem_ref[m : m + 1, pl.ds(pl.multiple_of(j * pair, 128), pair)]
            lane = q & 127
            which = q >> 7
            hot = one(jnp.broadcast_to(lane, (128, pair)) == iota((128, pair), 0))
            vals = mm(halves, hot)
            pick = jnp.broadcast_to(which, (rows, pair)) == iota((rows, pair), 0)
            owner = jnp.sum(jnp.where(pick, vals[:rows], 0.0), axis=0, keepdims=True)
            local = jnp.sum(jnp.where(pick, vals[rows:], 0.0), axis=0, keepdims=True)
            slot = owner * 32.0 + local
            s_ref[pl.ds(m * devs + 2 * j, 1), :] = slot[:, :per]
            s_ref[pl.ds(m * devs + 2 * j + 1, 1), :] = slot[:, per:]
            return 0

        lax.fori_loop(0, devs // 2, look, 0, unroll=4)

    tab_ref[...] = jnp.zeros((TAB_ROWS, 128), I32)
    slots = s_ref[...].astype(I32)
    mine = (slots >> 5) == me
    local = (slots & 31).astype(F32)
    upper = one(iota((per, per), 0) < iota((per, per), 1))
    before = mm(one(mine), upper)
    count = jnp.sum(jnp.where(mine, 1.0, 0.0), axis=1, keepdims=True)
    lead = jnp.concatenate([jnp.zeros((devs, 1), F32), count[:devs]], axis=0)
    rank = before + lead
    lower = one(iota((devs, devs), 1) < iota((devs, devs), 0))
    lane64 = iota((devs, 128), 1)
    carry = jnp.zeros((1, 128), F32)
    places, cells = [], []
    for r in range(CAP):
        hit = mine & (rank == float(r))
        got = jnp.sum(jnp.where(hit, local + 1.0, 0.0), axis=1, keepdims=True)
        got = got[:devs] + got[devs:]
        cell = jnp.where(got == 0.0, float(paths), got - 1.0).astype(I32)
        hot = jnp.broadcast_to(cell, (devs, 128)) == lane64
        within = mm(lower, one(hot)) + carry
        carry = carry + jnp.sum(jnp.where(hot, 1.0, 0.0), axis=0, keepdims=True)
        places.append(jnp.sum(jnp.where(hot, within, 0.0), axis=1, keepdims=True))
        cells.append(hot)
    lane1 = iota((1, 128), 1)
    groups = jnp.where(lane1 < paths, ((carry.astype(I32) + (GROUP - 1)) // GROUP).astype(F32), 0.0)
    strict = one(iota((128, 128), 0) < iota((128, 128), 1))
    start = mm(jnp.broadcast_to(groups.astype(BF16), (8, 128)), strict)[:1]
    end_col = to_col(start + groups, 128)
    ends = jnp.where(
        (jnp.broadcast_to(end_col, (128, 128)) <= iota((128, 128), 1).astype(F32))
        & (iota((128, 128), 0) < paths),
        1.0,
        0.0,
    )
    tab_ref[ROW_SLOT : ROW_SLOT + 1, :] = jnp.sum(ends, axis=0, keepdims=True).astype(I32)
    final = jnp.where(groups > 0.0, start + groups - 1.0, float(GROUPS))
    tab_ref[ROW_LAST : ROW_LAST + 1, :] = final.astype(I32)
    src_sum = jnp.zeros((16, 128), F32)
    rank_sum = jnp.zeros((16, 128), F32)
    link_sum = jnp.zeros((16, 128), F32)
    seen = jnp.zeros((16, 128), F32)
    source = iota((devs, 128), 0).astype(F32).astype(BF16)
    for r in range(CAP):
        first = jnp.sum(
            jnp.where(cells[r], jnp.broadcast_to(start, (devs, 128)), 0.0), axis=1, keepdims=True
        )
        real = jnp.sum(jnp.where(cells[r] & (lane64 < paths), 1.0, 0.0), axis=1, keepdims=True)
        pos = first * float(GROUP) + places[r]
        tab_ref[ROW_POS + r : ROW_POS + r + 1, :devs] = to_row(
            jnp.where(real > 0.0, pos, 0.0), devs
        ).astype(I32)
        pos = jnp.where(real > 0.0, pos.astype(I32), 1 << 20)
        high = one(jnp.broadcast_to(pos >> 7, (devs, 16)) == iota((devs, 16), 1))
        low = jnp.broadcast_to(pos & 127, (devs, 128)) == lane64
        src_sum = src_sum + mm_tn(high, jnp.where(low, source, jnp.zeros((), BF16)))
        found = mm_tn(high, one(low))
        rank_sum = rank_sum + found * float(r)
        link_sum = link_sum + found * float(r if r < HALF else r + (devs - 1) * HALF)
        seen = seen + found
    perm = jnp.where(seen > 0.0, src_sum * float(CAP) + rank_sum, float(devs * CAP))
    tab_ref[ROW_PERM : ROW_PERM + 10, :] = perm.astype(I32)[:10]
    perm = jnp.where(seen > 0.0, src_sum * float(HALF) + link_sum, float(devs * CAP))
    tab_ref[ROW_PERM_W : ROW_PERM_W + 10, :] = perm.astype(I32)[:10]

    own_ref[0:1, :] = s_ref[pl.ds(me, 1), :]
    own_ref[1:2, :] = s_ref[pl.ds(devs + me, 1), :]
    lower_g = one(iota((per, per), 1) < iota((per, per), 0))
    lane_g = iota((per, 128), 1)
    gene_col = iota((per, 128), 0).astype(F32).astype(BF16)
    carry = jnp.zeros((1, 128), F32)
    send = jnp.zeros((16, 128), F32)
    owner_rows = [own_ref[m : m + 1, :].astype(I32) >> 5 for m in range(2)]
    for m in range(2):
        owner = (to_col(own_ref[m : m + 1, :], per).astype(I32)) >> 5
        hot = jnp.broadcast_to(owner, (per, 128)) == lane_g
        within = mm(lower_g, one(hot)) + carry
        carry = carry + jnp.sum(jnp.where(hot, 1.0, 0.0), axis=0, keepdims=True)
        order = jnp.sum(jnp.where(hot, within, 0.0), axis=1, keepdims=True)
        cell = one(jnp.broadcast_to(order, (per, 16)) == iota((per, 16), 1).astype(F32))
        send = send + 2.0 * mm_tn(cell, jnp.where(hot, gene_col, jnp.zeros((), BF16)))
        if m:
            send = send + mm_tn(cell, one(hot))
        owner_row = owner_rows[m]
        order_row = to_row(order, per).astype(I32)
        put(tab_ref, ROW_RET + 2 * m, owner_row * CAP + order_row)
        link_row = owner_row * HALF + order_row
        link_row = jnp.where(order_row < HALF, link_row, link_row + (devs - 1) * HALF)
        put(tab_ref, ROW_LINK + 2 * m, link_row)
    tab_ref[ROW_SEND : ROW_SEND + CAP, :] = send.astype(I32)[:CAP]

    lens = len_ref[...].astype(F32) - 128.0
    starts = mm(jnp.broadcast_to(lens.astype(BF16), (8, per)), upper)[:1]
    starts = starts + 128.0 * iota((1, per), 1).astype(F32)
    start_col = jnp.broadcast_to(to_col(starts, per), (per, 256))
    begin = (iota((per, 256), 1) * COLS).astype(F32)
    inside = jnp.where(start_col <= begin, 1.0, 0.0)
    put(tab_ref, ROW_FIRST, (jnp.sum(inside, axis=0, keepdims=True) - 1.0).astype(I32))
    end = float(per * COLS)
    next_one = jnp.min(jnp.where(start_col > begin, start_col, end), axis=0, keepdims=True)
    next_two = jnp.min(
        jnp.where(start_col > jnp.broadcast_to(next_one, (per, 256)), start_col, end),
        axis=0, keepdims=True,
    )
    put(tab_ref, ROW_ONE, (next_one - begin[:1]).astype(I32))
    put(tab_ref, ROW_TWO, (next_two - begin[:1]).astype(I32))
    start_col = start_col[:, :per]
    starts_i = starts.astype(I32)
    last = (starts_i + len_ref[...] - 1) >> 8
    gene_row = iota((1, per), 1)
    for j in range(PARTS):
        block = (starts_i >> 8) + j
        edge = jnp.broadcast_to((block * COLS).astype(F32), (per, per))
        under = jnp.where(start_col <= edge, 1.0, 0.0)
        lead_gene = jnp.sum(under, axis=0, keepdims=True).astype(I32) - 1
        row = block * PARTS + (gene_row - lead_gene)
        put(tab_ref, ROW_PART + 2 * j, jnp.where(block <= last, row, per * PARTS))

    def relayout(e, _):
        at = pl.multiple_of(16 * e, 16)
        rows = link_ref[pl.ds(at, 16), :].astype(F32)
        for n in range(2):
            for t in range(8):
                tile_ref[pl.ds(64 * n + t, 8, stride=8), :] = rows[
                    8 * n : 8 * n + 8, 128 * t : 128 * t + 128
                ]
        for n in range(16):
            rows_ref[at + n] = tile_ref[8 * n : 8 * n + 8, :].astype(BF16)
        return 0

    lax.fori_loop(0, link_ref.shape[0] // 16, relayout, 0)


def look_up(tab_ref, row, index):
    return tab_ref[row + (index >> 7), index & 127]


def window_of(tab_ref, block):
    return tuple(look_up(tab_ref, row, block) for row in (ROW_FIRST, ROW_ONE, ROW_TWO))


def partner(me, k):
    off = lax.rem(k * STRIDE, 64)
    x = lax.rem(me // 16 + off // 16, 4)
    z = lax.rem((me // 4) % 4 + (off // 4) % 4, 4)
    y = lax.rem(me % 4 + off % 4, 4)
    return x * 16 + z * 4 + y


def greet(devs, me, core):
    barrier = pltpu.get_barrier_semaphore()

    def hello(k, _):
        pl.semaphore_signal(
            barrier, inc=1, device_id=(partner(me, k), core), device_id_type=MESH
        )
        return 0

    lax.fori_loop(1, devs, hello, 0, unroll=3)
    pl.semaphore_signal(barrier, inc=1, device_id=(me, 1 - core), device_id_type=MESH)
    pl.semaphore_wait(barrier, devs)


def load_chunks(src_ref, dst_ref, sem):
    return [
        pltpu.make_async_copy(
            src_ref.at[:, pl.ds(c * CHUNK, CHUNK)], dst_ref.at[:, pl.ds(c * CHUNK, CHUNK)], sem.at[c]
        )
        for c in range(src_ref.shape[1] // CHUNK)
    ]


def main_kernel(
    devs, genes, units, paths, punits,
    tab_ref, link_ref, head_ref, cot_ref, geno_ref, weight_ref,
    out_ref, lrow_ref, gh_ref,
    g_ref, gsib_ref, gw_ref, hid_ref, h_ref, w_ref, hs_ref, ws_ref, he_ref, wl_ref, gp_ref,
    hd_ref, delta_ref, heads_ref, own_gh, sib_gh, give_ref, take_ref, back_ref,
    own_ref, sib_ref, grad_ref, tile_ref,
    geno_sem, weight_sem, out_sem, hsend, hrecv, wsend, wrecv, dsend, drecv, lsend, lrecv, pair_sem,
):
    me = lax.axis_index("genes")
    core = lax.axis_index("batch")
    low = core * HALF
    high = (1 - core) * HALF
    samples = geno_ref.shape[0]
    half = units // 2
    tiles = punits // 8
    span = geno_ref.shape[1] // 2
    here = pl.multiple_of(core * span, span)
    there = pl.multiple_of((1 - core) * span, span)
    flat = pl.ds(0, (devs - 1) * CAP)
    flat_half = pl.ds(0, (devs - 1) * HALF)
    mine = core * (devs * HALF)
    loads = load_chunks(geno_ref, g_ref, geno_sem)
    weights = load_chunks(weight_ref, gw_ref, weight_sem)
    for weight, load in zip(weights, loads):
        weight.start()
        load.start()
    greet(devs, me, core)

    def send(src, dst, send_sem, recv_sem, to):
        return pltpu.make_async_remote_copy(
            src_ref=src, dst_ref=dst, send_sem=send_sem, recv_sem=recv_sem,
            device_id=(to, core), device_id_type=MESH,
        )

    def pair(src, dst, n):
        return pltpu.make_async_remote_copy(
            src_ref=src, dst_ref=dst, send_sem=pair_sem.at[2 * n], recv_sem=pair_sem.at[2 * n + 1],
            device_id=(me, 1 - core), device_id_type=MESH,
        )

    def w_step(k, _):
        to = partner(me, k)
        for r in range(HALF):
            ws_ref[to * HALF + r] = link_ref[tab_ref[low + r, to]]
        send(
            ws_ref.at[pl.ds(to * HALF, HALF)], w_ref.at[pl.ds(mine + me * HALF, HALF)],
            wsend, wrecv, to,
        ).start()
        return 0

    lax.fori_loop(1, devs, w_step, 0, unroll=3)

    pos = iota((units, COLS), 1)
    for n in range(2):
        gp_ref[2 * genes * PARTS + n] = jnp.zeros((8, 128), F32)
    per_chunk = CHUNK // COLS
    for c, load in enumerate(loads):
        weights[c].wait()
        load.wait()

        def block(i, _, c=c):
            for k in range(4):
                b = c * per_chunk + i * 4 + k
                _, one_end, two_end = window_of(tab_ref, b)
                cols = pl.ds(pl.multiple_of(b * COLS, COLS), COLS)
                weight = gw_ref[:, cols].astype(F32)
                not_one = pos >= one_end
                not_two = pos >= two_end
                zero = jnp.zeros_like(weight)
                basis = jnp.concatenate(
                    [
                        jnp.where(not_one, zero, weight),
                        jnp.where(not_one & jnp.logical_not(not_two), weight, zero),
                        jnp.where(not_two, weight, zero),
                    ],
                    axis=0,
                ).astype(BF16)
                got = mm_nt(basis, g_ref[:, cols])
                for w in range(2 * PARTS):
                    gp_ref[b * 2 * PARTS + w] = got[8 * w : 8 * w + 8]
            return 0

        lax.fori_loop(0, per_chunk // 4, block, 0)
    geno = pair(g_ref.at[:, pl.ds(there, span)], gsib_ref, 0)
    geno.start()

    def finish(i, _):
        for k in range(8):
            at = [2 * look_up(tab_ref, ROW_PART + 2 * j, i * 8 + k) for j in range(PARTS)]
            for n in range(2):
                total = gp_ref[at[0] + n] + gp_ref[at[1] + n] + gp_ref[at[2] + n]
                tile_ref[k * units + 8 * n : k * units + 8 * n + 8, :] = jnp.tanh(total)
        for k in range(8):
            even = tile_ref[pl.ds(k * units, half, stride=2), :]
            odd = tile_ref[pl.ds(k * units + 1, half, stride=2), :]
            hid_ref[i * 8 + k] = jnp.concatenate([even, odd], axis=1).astype(BF16)
        return 0

    lax.fori_loop(0, genes // 8, finish, 0)

    def h_step(k, _):
        to = partner(me, k)
        for r in range(CAP):
            hs_ref[to * CAP + r] = hid_ref[tab_ref[r, to] >> 1]
        send(
            hs_ref.at[pl.ds(to * CAP, CAP)], h_ref.at[pl.ds(me * CAP, CAP)], hsend, hrecv, to
        ).start()
        return 0

    lax.fori_loop(1, devs, h_step, 0, unroll=3)
    for r in range(CAP):
        h_ref[me * CAP + r] = hid_ref[tab_ref[r, me] >> 1]
    for r in range(HALF):
        w_ref[mine + me * HALF + r] = link_ref[tab_ref[low + r, me]]
    h_ref[devs * CAP] = jnp.zeros(h_ref.shape[1:], BF16)
    w_ref[devs * CAP] = jnp.zeros(w_ref.shape[1:], BF16)
    send(ws_ref.at[flat_half], w_ref.at[flat_half], wsend, wrecv, me).wait()
    part = w_ref.at[pl.ds(mine, devs * HALF)]
    share = pair(part, part, 8 + span // CHUNK)
    share.start()
    share.wait()

    def gather_w(i, _):
        for q in range(128 // GROUP):
            for j in range(GROUP):
                wl_ref[i * (128 // GROUP) + q, 8 * j : 8 * j + 8, :] = w_ref[
                    tab_ref[ROW_PERM_W + i, q * GROUP + j]
                ]
        return 0

    lax.fori_loop(0, GROUPS * GROUP // 128, gather_w, 0)
    heads_ref[...] = head_ref[...].astype(F32)
    for t in range(tiles):
        gp_ref[GROUPS * tiles + t] = jnp.zeros((8, 128), F32)
    delta_ref[paths] = jnp.zeros((punits, 128), BF16)
    for n in range(genes, own_ref.shape[0]):
        own_ref[n] = jnp.zeros((units, 128), BF16)
        sib_ref[n] = jnp.zeros((units, 128), BF16)
    send(hs_ref.at[flat], h_ref.at[flat], hsend, hrecv, me).wait()

    def up(i, carry):
        for q in range(128 // GROUP):
            c = i * (128 // GROUP) + q
            for j in range(GROUP):
                p = tab_ref[ROW_PERM + i, q * GROUP + j]
                he_ref[c, 8 * j : 8 * j + 8, :] = h_ref[p]
            out = mm_tn(wl_ref[c], he_ref[c])
            out = out[:punits, :128] + out[punits:, 128:]
            slot = tab_ref[ROW_SLOT, c]
            prev, total = carry
            total = out + jnp.where(slot == prev, total, jnp.zeros_like(total))
            for t in range(tiles):
                gp_ref[c * tiles + t] = total[8 * t : 8 * t + 8]
            carry = (slot, total)
        return carry

    lax.fori_loop(
        0, GROUPS * GROUP // 128, up, (jnp.full((), -1, I32), jnp.zeros((punits, 128), F32))
    )

    cot = cot_ref[...]
    lane = iota((punits, 128), 1)
    sub = iota((punits, 128), 0)

    def middle(i, _):
        row = jnp.zeros((1, 128), F32)
        head_row = heads_ref[pl.ds(i, 1), :]
        for n in range(2):
            s = 2 * i + n
            at = tab_ref[ROW_LAST, s] * tiles
            active = jnp.tanh(
                jnp.concatenate([gp_ref[at + t] for t in range(tiles)], axis=0)
            )
            diag = lane == sub + punits * n
            head = jnp.sum(
                jnp.where(diag, jnp.broadcast_to(head_row, (punits, 128)), 0.0),
                axis=1, keepdims=True,
            )
            grad = jnp.sum(active * cot, axis=1, keepdims=True)
            row = row + jnp.sum(
                jnp.where(diag, jnp.broadcast_to(grad, (punits, 128)), 0.0), axis=0, keepdims=True
            )
            delta_ref[s] = (cot * head * (1.0 - active * active)).astype(BF16)
        own_gh[pl.ds(i, 1), :] = row
        return 0

    lax.fori_loop(0, paths // 2, middle, 0)

    def wide_of(c):
        delta = delta_ref[tab_ref[ROW_SLOT, c]]
        none = jnp.zeros_like(delta)
        return jnp.concatenate(
            [
                jnp.concatenate([delta, none], axis=1),
                jnp.concatenate([none, delta], axis=1),
            ],
            axis=0,
        )

    def down(i, _):
        for q in range(4):
            c = i * 4 + q
            hd = mm(wl_ref[c], wide_of(c)).astype(BF16)
            for j in range(GROUP):
                hd_ref[c * GROUP + j] = hd[8 * j : 8 * j + 8]
        return 0

    lax.fori_loop(0, GROUPS // 4, down, 0)

    def d_step(k, _):
        to = partner(me, k)
        for r in range(CAP):
            hs_ref[to * CAP + r] = hd_ref[tab_ref[ROW_POS + r, to]]
        send(
            hs_ref.at[pl.ds(to * CAP, CAP)], back_ref.at[pl.ds(me * CAP, CAP)], dsend, drecv, to
        ).start()
        return 0

    lax.fori_loop(1, devs, d_step, 0, unroll=3)

    def down_links(i, _):
        for q in range(4):
            c = i * 4 + q
            gp = mm_nt(he_ref[c], wide_of(c))
            for j in range(GROUP):
                gp_ref[c * GROUP + j] = gp[8 * j : 8 * j + 8]
        return 0

    lax.fori_loop(0, GROUPS // 4, down_links, 0)

    def give_step(i, _):
        for r in range(HALF):
            give_ref[i * HALF + r] = gp_ref[tab_ref[ROW_POS + high + r, i]]
        return 0

    lax.fori_loop(0, devs, give_step, 0)
    parts = pair(give_ref, take_ref, 1)
    parts.start()
    swap = pair(own_gh, sib_gh, 2)
    swap.start()
    for r in range(CAP):
        back_ref[me * CAP + r] = hd_ref[tab_ref[ROW_POS + r, me]]
    parts.wait()

    def l_step(k, _):
        to = partner(me, k)
        for r in range(HALF):
            ws_ref[to * HALF + r] = (
                gp_ref[tab_ref[ROW_POS + low + r, to]] + take_ref[to * HALF + r]
            ).astype(BF16)
        send(
            ws_ref.at[pl.ds(to * HALF, HALF)], lrow_ref.at[pl.ds(mine + me * HALF, HALF)],
            lsend, lrecv, to,
        ).start()
        return 0

    lax.fori_loop(1, devs, l_step, 0)
    for r in range(HALF):
        lrow_ref[mine + me * HALF + r] = (
            gp_ref[tab_ref[ROW_POS + low + r, me]] + take_ref[me * HALF + r]
        ).astype(BF16)
    swap.wait()
    gh_ref[...] = own_gh[...] + sib_gh[...]
    send(hs_ref.at[flat], back_ref.at[flat], dsend, drecv, me).wait()

    def gene(i, _):
        for k in range(4):
            g = 4 * i + k
            a = look_up(tab_ref, ROW_RET, g)
            b = look_up(tab_ref, ROW_RET + 2, g)
            both = back_ref[a].astype(F32) + back_ref[b].astype(F32)
            hid = hid_ref[g].astype(F32)
            value = both * (1.0 - hid * hid)
            tile_ref[pl.ds(k * units, half, stride=2), :] = value[:, :128]
            tile_ref[pl.ds(k * units + 1, half, stride=2), :] = value[:, 128:]
        for k in range(4):
            own_ref[4 * i + k] = tile_ref[k * units : (k + 1) * units, :].astype(BF16)
        return 0

    quarter = genes // 4
    deltas = []
    for n in range(4):
        lax.fori_loop(n * quarter // 4, (n + 1) * quarter // 4, gene, 0)
        rows = pl.ds(n * quarter, quarter)
        delta = pair(own_ref.at[rows], sib_ref.at[rows], 4 + n)
        delta.start()
        deltas.append(delta)
    geno.wait()
    for delta in deltas:
        delta.wait()

    stores = []
    first_block = core * (span // COLS)
    for c in range(span // CHUNK):
        def block(i, _, c=c):
            for k in range(4):
                b = c * per_chunk + i * 4 + k
                first, one_end, two_end = window_of(tab_ref, first_block + b)
                left = jnp.concatenate(
                    [
                        jnp.concatenate([ref[first + w] for w in range(PARTS)], axis=0)
                        for ref in (own_ref, sib_ref)
                    ],
                    axis=1,
                )
                cols = pl.ds(pl.multiple_of(b * COLS, COLS), COLS)
                whole = pl.ds(pl.multiple_of(here + b * COLS, COLS), COLS)
                right = jnp.concatenate([g_ref[:, whole], gsib_ref[:, cols]], axis=0)
                full = mm(left, right)
                grad_ref[:, cols] = jnp.where(
                    pos >= two_end,
                    full[2 * units :],
                    jnp.where(pos >= one_end, full[units : 2 * units], full[:units]),
                )
            return 0

        lax.fori_loop(0, per_chunk // 4, block, 0)
        cols = pl.ds(pl.multiple_of(here + c * CHUNK, CHUNK), CHUNK)
        piece = grad_ref.at[:, pl.ds(c * CHUNK, CHUNK)]
        store = pltpu.make_async_copy(piece, out_ref.at[:, cols], out_sem.at[c])
        store.start()
        stores.append(store)
        store = pair(piece, out_ref.at[:, cols], 8 + c)
        store.start()
        stores.append(store)

    send(ws_ref.at[flat_half], lrow_ref.at[flat_half], lsend, lrecv, me).wait()
    part = lrow_ref.at[pl.ds(mine, devs * HALF)]
    share = pair(part, part, 3)
    share.start()
    share.wait()

    for store in stores:
        store.wait()


def final_kernel(
    tab_ref, link_hbm, grad_ref, head_ref, out_ref, path_ref, gh_ref,
    link_ref, piece_ref, rows_ref, tile_ref, link_sem, in_sem, out_sem, path_sem,
):
    pieces = in_sem.shape[0]
    links = path_ref.shape[0]
    per = links // pieces
    fetch = pltpu.make_async_copy(link_hbm, link_ref, link_sem)
    fetch.start()
    reads = load_chunks(grad_ref, piece_ref, in_sem)
    for read in reads:
        read.start()
    gh_ref[...] = head_ref[...]
    fetch.wait()
    writes = []
    for c in range(pieces):

        for n in range(per // 8):
            for j in range(8):
                e = c * per // 8 + n
                at = look_up(tab_ref, ROW_LINK + 2 * (j % 2), e * 4 + j // 2)
                tile_ref[64 * n + 8 * j : 64 * n + 8 * j + 8, :] = link_ref[at].astype(F32)
        for n in range(per // 8):
            e = c * per // 8 + n
            for t in range(8):
                rows_ref[8 * e : 8 * e + 8, 128 * t : 128 * t + 128] = tile_ref[
                    pl.ds(64 * n + t, 8, stride=8), :
                ]
        rows = pl.ds(c * per, per)
        writes.append(pltpu.make_async_copy(rows_ref.at[rows], path_ref.at[rows], path_sem.at[c]))
        writes[-1].start()
        reads[c].wait()
        cols = pl.ds(c * CHUNK, CHUNK)
        writes.append(
            pltpu.make_async_copy(piece_ref.at[:, cols], out_ref.at[:, cols], out_sem.at[c])
        )
        writes[-1].start()
    for write in writes:
        write.wait()


def vmem():
    return pl.BlockSpec(memory_space=pltpu.VMEM)


def smem():
    return pl.BlockSpec(memory_space=pltpu.SMEM)


def hbm():
    return pl.BlockSpec(memory_space=pl.ANY)


LIMIT = 60 * 1024 * 1024


def on_device(
    genotypes, gene_weight, gene_lengths, membership, pathway_slot, pathway_weight,
    head_weight, cotangent,
):
    devs = lax.axis_size("genes")
    genes = gene_lengths.shape[0]
    links = pathway_weight.shape[0]
    units = gene_weight.shape[0]
    samples, variants = genotypes.shape
    punits = pathway_weight.shape[1] // units
    paths = head_weight.shape[0] // punits
    half = units // 2
    shape = jax.ShapeDtypeStruct

    tab, link_rows = pl.pallas_call(
        functools.partial(index_kernel, devs, genes, paths),
        out_shape=(
            shape((TAB_ROWS, 128), I32),
            shape((links, half, 2 * punits), BF16),
        ),
        in_specs=[vmem()] * 4,
        out_specs=(vmem(),) * 2,
        scratch_shapes=[
            pltpu.VMEM((2 * devs, genes), F32),
            pltpu.VMEM((2, genes), F32),
            pltpu.VMEM((128, 128), F32),
        ],
        compiler_params=pltpu.CompilerParams(vmem_limit_bytes=LIMIT),
        name="index",
    )(membership.T, pathway_slot.reshape(-1, 128), gene_lengths.reshape(1, -1), pathway_weight)

    pieces = variants // CHUNK
    sem = pltpu.SemaphoreType.DMA
    heads = (paths * punits // 128, 128)
    tile = lambda n, width, kind: pltpu.VMEM((n, half, width), kind)
    grad_parts, link_parts, head_parts = pl.pallas_call(
        functools.partial(main_kernel, devs, genes, units, paths, punits),
        out_shape=(
            shape((units, variants), F32),
            shape((devs * CAP, half, 2 * punits), BF16),
            shape(heads, F32),
        ),
        in_specs=[smem()] + [vmem()] * 3 + [hbm()] * 2,
        out_specs=(hbm(), vmem(), vmem()),
        scratch_shapes=[
            pltpu.VMEM((samples, variants), BF16),
            pltpu.VMEM((samples, variants // 2), BF16),
            pltpu.VMEM((units, variants), BF16),
            tile(genes, 2 * samples, BF16),
            tile(devs * CAP + 1, 2 * samples, BF16),
            tile(devs * CAP + 1, 2 * punits, BF16),
            tile(devs * CAP, 2 * samples, BF16),
            tile(devs * HALF, 2 * punits, BF16),
            pltpu.VMEM((GROUPS, half * GROUP, 2 * samples), BF16),
            pltpu.VMEM((GROUPS, half * GROUP, 2 * punits), BF16),
            tile(GROUPS * GROUP, 2 * punits, F32),
            tile(GROUPS * GROUP, 2 * samples, BF16),
            pltpu.VMEM((paths + 1, punits, samples), BF16),
            pltpu.VMEM(heads, F32),
            pltpu.VMEM(heads, F32),
            pltpu.VMEM(heads, F32),
            tile(devs * HALF, 2 * punits, F32),
            tile(devs * HALF, 2 * punits, F32),
            tile(devs * CAP, 2 * samples, BF16),
            pltpu.VMEM((genes + 2, units, samples), BF16),
            pltpu.VMEM((genes + 2, units, samples), BF16),
            pltpu.VMEM((units, variants // 2), F32),
            pltpu.VMEM((8 * units, samples), F32),
        ]
        + [sem((pieces,))] * 2
        + [sem((pieces // 2,))]
        + [sem(())] * 8
        + [sem((18 + pieces,))],
        compiler_params=pltpu.CompilerParams(
            collective_id=0, has_side_effects=True, vmem_limit_bytes=66_000_000
        ),
        name="main",
    )(
        tab,
        link_rows,
        head_weight.reshape(-1, 128),
        cotangent.reshape(1, -1),
        genotypes,
        gene_weight,
    )
    grad_gene, grad_pathway, grad_head = pl.pallas_call(
        final_kernel,
        out_shape=(
            shape((units, variants), F32),
            shape((links, units * punits), F32),
            shape(heads, F32),
        ),
        in_specs=[smem(), hbm(), hbm(), vmem()],
        out_specs=(hbm(), hbm(), vmem()),
        scratch_shapes=[
            pltpu.VMEM(link_parts.shape, BF16),
            pltpu.VMEM((units, variants), F32),
            pltpu.VMEM((links, units * punits), F32),
            pltpu.VMEM((links // pieces * half, 2 * punits), F32),
            sem(()),
            sem((pieces,)),
            sem((pieces,)),
            sem((pieces,)),
        ],
        compiler_params=pltpu.CompilerParams(vmem_limit_bytes=LIMIT),
        name="final",
    )(tab, link_parts, grad_parts, head_parts)
    return grad_gene, grad_pathway, grad_head.reshape(-1)


def solution(mesh):
    return jax.shard_map(
        on_device,
        mesh=mesh,
        in_specs=(
            P("batch", "genes"), P(None, "genes"), P("genes"), P(), P(),
            P("genes", None), P("genes"), P("batch"),
        ),
        out_specs=(P(None, "genes"), P("genes", None), P("genes")),
        check_vma=False,
    )
```
